128 devices in a mesh: row: 8 (over y, core), col: 16 (over x, z).
Axes of the slice: x: 4, y: 4, z: 4, core: 2. Of those that a mesh axis runs over, the one named last changes fastest.
Arguments:
- marginal: float32 [131072, 128], P(('row', 'col')), may hold values from -6 to 6
- penalty: float32 [128], replicated, may hold values from 0.5 to 8
- ld_diag: float32 [128, 1024, 1024], P(('row', 'col')), may hold values from -0.005 to 1, as said below
- ld_low: float32 [128, 2, 1024, 1024], P(('row', 'col')), may hold values from -0.006 to 0.36
- band: int32 [128], P(('row', 'col')), may hold values from 0 to 2
- genotypes: bfloat16 [5120, 131072], P(None, ('row', 'col')), may hold values from -5 to 5
Outputs:
- effects: float32 [131072, 128], P(('row', 'col'))
- scores: float32 [5120, 128], P(('row', 'col'))
The draws below stay inside these ranges and needn't reach their ends.
Inputs may be any that keep to these rules, and one draw needn't show every extreme that they name: Each block of ld_diag is symmetric with ones on its diagonal.
All inputs are finite; a program needn't handle non-finite values.
Results may differ from the reference program's by a relative error of at most 0.0023.
The reference program's roundings to bfloat16 on the way (of `rounded`) count: a program that leaves them out, or rounds other values in their place, can miss the bound.
Values sent between devices are 32-bit elements; how exact they have to be, the bound alone decides.
A program may use at most 128 MiB of HBM per device.

```python
import math
import jax
import jax.numpy as jnp
from jax import lax

BS = 1024
K = 128
ITERS = 3
NB = 128
M = 131072
PEOPLE = 5120


def block_shape(key):
    lower_gap = 0.02
    upper_gap = 0.05
    fraction = jax.random.uniform(jax.random.fold_in(key, 11), (NB,), jnp.float32)
    gaps = jnp.exp(jnp.log(lower_gap) + fraction * (jnp.log(upper_gap) - jnp.log(lower_gap)))
    decays = 1.0 - gaps
    corner = jax.random.uniform(jax.random.fold_in(key, 12), (NB,), jnp.float32, 0.1, 0.35)
    return (decays, corner)


def draw_ld_diag(key, part):
    decays, corner = block_shape(key)
    positions = jnp.arange(BS, dtype=jnp.float32)
    distance = jnp.abs(positions[:, None] - positions[None, :])
    smooth = jnp.power(decays[:, None, None], distance[None, :, :])
    spread = jax.random.uniform(jax.random.fold_in(key, 21), (NB, BS, BS), jnp.float32, -1.0, 1.0)
    factor = 0.004
    symmetric = (spread + jnp.swapaxes(spread, 1, 2)) * (0.5 * factor)
    combined = smooth + symmetric
    return jnp.where(distance[None, :, :] < 0.5, jnp.float32(1.0), combined)


def draw_ld_low(key, part):
    decays, corner = block_shape(key)
    previous = jnp.roll(decays, 1)
    positions = jnp.arange(BS, dtype=jnp.float32)
    row_decay = jnp.power(decays[:, None], positions[None, :])
    col_decay = jnp.power(previous[:, None], (BS - positions)[None, :])
    coupled = corner[:, None, None] * row_decay[:, :, None] * col_decay[:, None, :]
    noise_one = jax.random.uniform(jax.random.fold_in(key, 31), (NB, BS, BS), jnp.float32, -0.003, 0.003)
    noise_two = jax.random.uniform(jax.random.fold_in(key, 32), (NB, BS, BS), jnp.float32, -0.006, 0.006)
    return jnp.stack([coupled + noise_one, noise_two], axis=1)


def place_ends(array, own_key, smallest, largest):
    index_at = [jax.random.randint(jax.random.fold_in(own_key, axis), (), 0, length) for axis, length in enumerate(array.shape)]
    main_axis = array.shape.index(max(array.shape))
    beside = index_at[:main_axis] + [(index_at[main_axis] + 1) % array.shape[main_axis]] + index_at[main_axis + 1:]
    return array.at[tuple(index_at)].set(smallest).at[tuple(beside)].set(largest)


def shard_levels(key, dims, shards, low, largest):
    def one(dim, shards_of):
        draws = jax.random.uniform(jax.random.fold_in(jax.random.fold_in(key, 6), dim), (shards_of,), jnp.float32, low / len(shards), largest / len(shards))
        return jnp.repeat(jnp.exp(draws), dims[dim] // shards_of).reshape((-1,) + (1,) * (len(dims) - dim - 1))

    level = one(*shards[0])
    for cut in shards[1:]:
        level = level * one(*cut)
    return level


def gaussian(rng, dims, scale, reach, split=(), kind=jnp.bfloat16):
    result = jax.random.normal(rng, dims, jnp.float32) * scale
    if len(split) > 0:
        result = shard_levels(rng, dims, split, -0.22, 0.18) * result
    return jnp.clip(result, min=-reach, max=reach).astype(kind)


def setup_inputs(seed: int = 0) -> dict:
    key_of = jax.random.split(jax.random.key(seed), 7)
    marginal = gaussian(key_of[0], (M, K), 1.0, 6.0, ((0, 128),), jnp.float32)
    penalty = jnp.clip(jnp.exp(jax.random.uniform(key_of[1], (K,), jnp.float32, math.log(0.5), math.log(8.0))), 0.5, 8.0)
    ld_diag = draw_ld_diag(jax.random.fold_in(key_of[6], 71), 0)
    ld_low = draw_ld_low(jax.random.fold_in(key_of[6], 71), 0)
    band = place_ends(jax.random.randint(key_of[4], (NB,), 0, 3), jax.random.fold_in(key_of[4], 1), 0, 2).astype(jnp.int32)
    genotypes = gaussian(key_of[5], (PEOPLE, M), 1.0, 5.0, ((1, 128),))
    return dict(marginal=marginal, penalty=penalty, ld_diag=ld_diag, ld_low=ld_low, band=band, genotypes=genotypes)


def apply_operator(vec, ld_diag, ld_low, band, penalty):
    hp = lax.Precision.HIGHEST
    out = jnp.einsum("nij,njk->nik", ld_diag, vec, precision=hp) + penalty * vec
    blocks = jnp.arange(NB)
    for dist in (1, 2):
        active = jnp.logical_and(band >= dist, blocks >= dist).astype(jnp.float32)
        tile = ld_low[:, dist - 1] * active[:, None, None]
        below = jnp.concatenate([jnp.zeros((dist, BS, K), jnp.float32), vec[:-dist]], axis=0)
        out = out + jnp.einsum("nij,njk->nik", tile, below, precision=hp)
        upper = jnp.einsum("nji,njk->nik", tile, vec, precision=hp)
        out = out + jnp.concatenate([upper[dist:], jnp.zeros((dist, BS, K), jnp.float32)], axis=0)
    return out


def reference(marginal, penalty, ld_diag, ld_low, band, genotypes):
    residual = marginal.reshape(NB, BS, K)
    direction = residual
    effects = jnp.zeros_like(residual)
    norm_now = jnp.sum(residual * residual, axis=(0, 1))
    for step in range(ITERS):
        image = apply_operator(direction, ld_diag, ld_low, band, penalty)
        alpha = norm_now / jnp.sum(direction * image, axis=(0, 1))
        effects = effects + alpha * direction
        residual = residual - alpha * image
        norm_next = jnp.sum(residual * residual, axis=(0, 1))
        direction = residual + (norm_next / norm_now) * direction
        norm_now = norm_next
    effects = effects.reshape(M, K)
    rounded = effects.astype(jnp.bfloat16)
    scores = jnp.dot(genotypes, rounded, preferred_element_type=jnp.float32)
    return effects, scores
```

```python
import functools

import jax
import jax.numpy as jnp
from jax import lax
from jax.experimental import pallas as pl
from jax.experimental.pallas import tpu as pltpu
from jax.sharding import PartitionSpec as P

MESH = pl.DeviceIdType.MESH
F32 = jnp.float32
BF16 = jnp.bfloat16
BS = 1024
K = 128
ROWS = 8
COLS = 16
CH = 256
NC = BS // CH
HALF = BS // 2
GROUP = 640
PARTS = ((0, 16, "yzx"), (16, 16, "zxy"), (32, 8, "xyz"))


def split(v):
    high = v.astype(BF16)
    return high, (v - high.astype(F32)).astype(BF16)


def both(v):
    return jnp.concatenate(split(v), axis=1)


def dot(a, b):
    return jnp.dot(a, b, preferred_element_type=F32)


def product(high, low, pair):
    wide = dot(high, pair)
    return wide[:, :K] + wide[:, K:] + dot(low, pair[:, :K])


def chunk(c):
    return pl.ds(pl.multiple_of(c * CH, CH), CH)


def kernel(
    mask, b, penalty, ld_diag, ld_low, genotypes,
    effects, scores,
    stage, tiles, flipped, geno, vec, m1, m2, pair, u2, ru2, us, rus, look, dw,
    q1, r1, d1, d2, x01, rounded, payload, ar_one, ar_two, mid,
    sc, rc, total, p0a, p0b, p0c, p1a, p1b, p1c, p2a, p2b, p2c, v0, v1, v2, w0, w1, w2,
    load_sem, geno_sem, chain_s, chain_r, ar_s, ar_r, core_s, core_r, rs_s, rs_r,
):
    row, col = lax.axis_index("row"), lax.axis_index("col")
    place = row * COLS + col
    y, core, x, z = row // 2, row % 2, col // 4, col % 4

    def hop(distance):
        to = (place + distance + ROWS * COLS) % (ROWS * COLS)
        return (to // COLS, to % COLS)

    def at(**new):
        p = dict(y=y, core=core, x=x, z=z)
        p.update(new)
        return (p["y"] * 2 + p["core"], p["x"] * 4 + p["z"])

    def load(t, h):
        n = 2 * t + h
        src = ld_diag.at[0] if t == 2 else ld_low.at[0, 1 - t]
        return pltpu.make_async_copy(
            src.at[pl.ds(h * HALF, HALF)], stage.at[n % 2], load_sem.at[n % 2]
        )

    load(0, 0).start()
    load(0, 1).start()
    geno_copy = pltpu.make_async_copy(genotypes, geno, geno_sem)

    barrier = pltpu.get_barrier_semaphore()
    for distance in (1, 2, -1, -2):
        pl.semaphore_signal(barrier, inc=1, device_id=hop(distance), device_id_type=MESH)

    @pl.loop(1, COLS)
    def _(k):
        pl.semaphore_signal(barrier, inc=1, device_id=(row, (col + k) % COLS), device_id_type=MESH)

    @pl.loop(1, ROWS)
    def _(k):
        pl.semaphore_signal(barrier, inc=1, device_id=((row + k) % ROWS, col), device_id_type=MESH)

    pl.semaphore_wait(barrier, 4 + COLS - 1 + ROWS - 1)

    def remote(src, dst, send, recv, device):
        return pltpu.make_async_remote_copy(
            src_ref=src, dst_ref=dst, send_sem=send, recv_sem=recv,
            device_id=device, device_id_type=MESH,
        )

    def source(e):
        return b if e == 0 else vec.at[e - 1]

    def send_own(e, c):
        return remote(source(e).at[chunk(c)], m1.at[e, chunk(c)],
                      chain_s.at[e, 0, c], chain_r.at[e, 0, c], hop(1))

    def send_on(e, c):
        return remote(m1.at[e, chunk(c)], m2.at[e, chunk(c)],
                      chain_s.at[e, 1, c], chain_r.at[e, 1, c], hop(1))

    def send_u2(e, c):
        return remote(u2.at[e, chunk(c)], ru2.at[e, chunk(c)],
                      chain_s.at[e, 2, c], chain_r.at[e, 2, c], hop(-1))

    def send_us(e, c):
        return remote(us.at[e, chunk(c)], rus.at[e, chunk(c)],
                      chain_s.at[e, 3, c], chain_r.at[e, 3, c], hop(-1))

    @pl.loop(0, NC)
    def _(c):
        send_own(0, c).start()

    def convert(t):
        for h in range(2):
            load(t, h).wait()
            n = 2 * t + h

            @pl.loop(0, HALF // CH)
            def _(c):
                block = stage[n % 2, chunk(c), :]
                if t < 2:
                    block = block * mask[1 - t]
                rows = pl.ds(pl.multiple_of(h * HALF + c * CH, CH), CH)
                high, low = split(block)
                tiles[t, 0, rows, :] = high
                tiles[t, 1, rows, :] = low
                if t < 2:
                    high, low = split(block.T)
                    flipped[t, 0, :, rows] = high
                    flipped[t, 1, :, rows] = low

            if t < 2:
                load(t + 1, h).start()

    def ar_col(n, k):
        return remote(payload.at[n], ar_one.at[n, k], ar_s.at[n, 0, k], ar_r.at[n, 0, k],
                      (row, (col + k) % COLS))

    def ar_row(n, k):
        return remote(mid.at[n], ar_two.at[n, k], ar_s.at[n, 1, k], ar_r.at[n, 1, k],
                      ((row + k) % ROWS, col))

    def ar_start(n, rows):
        for j in range(8):
            payload[n, j : j + 1, :] = rows[j] if j < len(rows) else jnp.zeros((1, K), F32)

        @pl.loop(1, COLS)
        def _(k):
            ar_col(n, k).start()

    def ar_middle(n):
        @pl.loop(1, COLS)
        def _(k):
            ar_col(n, k).wait_recv()

        acc = payload[n]
        for k in range(1, COLS):
            acc = acc + ar_one[n, k]
        mid[n] = acc

        @pl.loop(1, ROWS)
        def _(k):
            ar_row(n, k).start()

    def ar_end(n):
        @pl.loop(1, ROWS)
        def _(k):
            ar_row(n, k).wait_recv()

        acc = mid[n]
        for k in range(1, ROWS):
            acc = acc + ar_two[n, k]
        return acc

    def column(v):
        return jnp.sum(v, axis=0, keepdims=True)

    def over_chunks(body, count):
        zero = jnp.zeros((1, K), F32)
        return lax.fori_loop(0, NC, body, (zero,) * count)

    def exchange(e, last, early, late):
        src = source(e)

        @pl.loop(0, NC)
        def _(c):
            pair[chunk(c), :] = both(src[chunk(c), :])

        early()
        if e == 0:
            convert(0)
        if not last:
            @pl.loop(0, NC)
            def _(c):
                u2[e, chunk(c), :] = product(flipped[0, 0, chunk(c), :], flipped[0, 1, chunk(c), :], pair[...])
                send_u2(e, c).start()

        if e == 0:
            convert(1)

        @pl.loop(0, NC)
        def _(c):
            send_own(e, c).wait_recv()
            send_on(e, c).start()
            there = both(m1[e, chunk(c), :])
            for r in range(NC):
                rows = pl.ds(r * CH, CH)
                part = product(tiles[1, 0, rows, chunk(c)], tiles[1, 1, rows, chunk(c)], there)
                part = jnp.where(c == 0, part, part + look[e, rows, :])
                look[e, rows, :] = part
            if not last:
                up = product(flipped[1, 0, chunk(c), :], flipped[1, 1, chunk(c), :], pair[...])
                send_u2(e, c).wait_recv()
                us[e, chunk(c), :] = up + ru2[e, chunk(c), :]
                send_us(e, c).start()

        if e == 0:
            convert(2)

        @pl.loop(0, NC)
        def _(c):
            dw[chunk(c), :] = (
                product(tiles[2, 0, chunk(c), :], tiles[2, 1, chunk(c), :], pair[...])
                + penalty[...] * src[chunk(c), :]
            )

        late()

        @pl.loop(0, NC)
        def _(c):
            send_on(e, c).wait_recv()
            there = both(m2[e, chunk(c), :])
            for r in range(NC):
                rows = pl.ds(r * CH, CH)
                look[e, rows, :] += product(tiles[0, 0, rows, chunk(c)], tiles[0, 1, rows, chunk(c)], there)

    def finish(e, c):
        down = look[e, chunk(c), :]
        mine = dw[chunk(c), :]
        send_us(e, c).wait_recv()
        out = mine + down + rus[e, chunk(c), :]
        look[e, chunk(c), :] = mine + 2.0 * down
        vec[e, chunk(c), :] = out
        send_own(e + 1, c).start()
        return out

    exchange(0, False, lambda: None, lambda: None)
    geno_copy.start()

    def one(c, sums):
        out = finish(0, c)
        here = b[chunk(c), :]
        return (sums[0] + column(here * here), sums[1] + column(here * out), sums[2] + column(out * out))

    sums_one = over_chunks(one, 3)

    coef = {}

    def solve_one():
        got = ar_end(0)
        bb, bq, qq = got[0:1], got[1:2], got[2:3]
        alpha = bb / bq
        after = jnp.maximum(bb - 2.0 * alpha * bq + alpha * alpha * qq, 0.0)
        coef["a0"], coef["b1"] = alpha, after / bb

    def early_one():
        ar_start(0, sums_one)

    def late_one():
        ar_middle(0)
        solve_one()

    exchange(1, False, early_one, late_one)
    a0, b1 = coef["a0"], coef["b1"]

    def two(c, sums):
        s = finish(1, c)
        here, q = b[chunk(c), :], vec[0, chunk(c), :]
        res = here - a0 * q
        direction = res + b1 * here
        image = (1.0 + b1) * q - a0 * s
        r1[chunk(c), :] = res
        d1[chunk(c), :] = direction
        q1[chunk(c), :] = image
        terms = (res * res, res * direction, direction * image, res * image, image * image)
        return tuple(t + column(v) for t, v in zip(sums, terms))

    sums_two = over_chunks(two, 5)

    def early_two():
        ar_start(1, sums_two)

    def late_two():
        ar_middle(1)
        got = ar_end(1)
        rr, rd, dq, rq, qq = (got[j : j + 1] for j in range(5))
        alpha = rd / dq
        after = jnp.maximum(rr - 2.0 * alpha * rq + alpha * alpha * qq, 0.0)
        beta = after / rr
        coef["a1"], coef["b2"] = alpha, beta

        def body(c, sums):
            res = r1[chunk(c), :] - alpha * q1[chunk(c), :]
            direction = res + beta * d1[chunk(c), :]
            d2[chunk(c), :] = direction
            x01[chunk(c), :] = a0 * b[chunk(c), :] + alpha * d1[chunk(c), :]
            return (sums[0] + column(res * direction),)

        coef["rd2"] = over_chunks(body, 1)[0]

    exchange(2, True, early_two, late_two)
    a1, b2 = coef["a1"], coef["b2"]
    c0 = 1.0 + b2 * (1.0 + b1)
    c1 = -a0 - a1 * (1.0 + b1) - b2 * a0
    c2 = a1 * a0

    def three(c, sums):
        third = dw[chunk(c), :] + 2.0 * look[2, chunk(c), :]
        image = c0 * look[0, chunk(c), :] + c1 * look[1, chunk(c), :] + c2 * third
        return (sums[0] + column(d2[chunk(c), :] * image),)

    dq2 = over_chunks(three, 1)[0]
    ar_start(2, (coef["rd2"], dq2))
    geno_copy.wait()
    ar_middle(2)
    got = ar_end(2)
    a2 = got[0:1] / got[1:2]

    @pl.loop(0, NC)
    def _(c):
        value = x01[chunk(c), :] + a2 * d2[chunk(c), :]
        effects[chunk(c), :] = value
        rounded[chunk(c), :] = value.astype(BF16)

    def people(j, which):
        rows = pl.ds(pl.multiple_of((j * 2 + which) * GROUP, GROUP), GROUP)
        return dot(geno[rows, :], rounded[...]).reshape(4, 4, 40, K)

    def core_copy(j):
        return remote(sc.at[j], rc.at[j], core_s.at[j], core_r.at[j], at(core=1 - core))

    @pl.loop(0, 4)
    def _(j):
        sc[j] = people(j, 1 - core)
        core_copy(j).start()

    @pl.loop(0, 4)
    def _(j):
        mine = people(j, core)
        core_copy(j).wait_recv()
        total[j] = mine + rc[j]

    def axis_copy(step, part, k):
        start, size, order = PARTS[part]
        axis = order[step]
        mine = dict(y=y, x=x, z=z)[axis]
        to = (mine + k) % 4
        dst = ((p0a, p0b, p0c), (p1a, p1b, p1c), (p2a, p2b, p2c))[part][step].at[k - 1]
        if step == 0:
            rows = pl.ds(start, size)
            src = {"y": lambda: total.at[to, :, :, rows, :],
                   "x": lambda: total.at[:, to, :, rows, :],
                   "z": lambda: total.at[:, :, to, rows, :]}[axis]()
        elif step == 1:
            left = [a for a in "yxz" if a != order[0]]
            ref = (v0, v1, v2)[part]
            src = ref.at[to] if left[0] == axis else ref.at[:, to]
        else:
            src = (w0, w1, w2)[part].at[to]
        return remote(src, dst, rs_s.at[step, part, k], rs_r.at[step, part, k], at(**{axis: to}))

    for step in range(3):
        for k in (1, 3, 2):
            for part in range(3):
                axis_copy(step, part, k).start()
        for part in range(3):
            start, size, order = PARTS[part]
            axis = order[step]
            mine = dict(y=y, x=x, z=z)[axis]
            rows = pl.ds(start, size)
            if step == 0:
                acc = {"y": lambda: total[mine, :, :, rows, :],
                       "x": lambda: total[:, mine, :, rows, :],
                       "z": lambda: total[:, :, mine, rows, :]}[axis]()
            elif step == 1:
                left = [a for a in "yxz" if a != order[0]]
                ref = (v0, v1, v2)[part]
                acc = ref[mine] if left[0] == axis else ref[:, mine]
            else:
                acc = (w0, w1, w2)[part][mine]
            got = ((p0a, p0b, p0c), (p1a, p1b, p1c), (p2a, p2b, p2c))[part][step]
            for k in (1, 3, 2):
                axis_copy(step, part, k).wait_recv()
                acc = acc + got[k - 1]
            if step == 0:
                (v0, v1, v2)[part][...] = acc
            elif step == 1:
                (w0, w1, w2)[part][...] = acc
            else:
                scores[rows, :] = acc

    for e in range(3):
        @pl.loop(0, NC)
        def _(c):
            send_own(e, c).wait_send()
            send_on(e, c).wait_send()
            if e < 2:
                send_u2(e, c).wait_send()
                send_us(e, c).wait_send()

        @pl.loop(1, COLS)
        def _(k):
            ar_col(e, k).wait_send()

        @pl.loop(1, ROWS)
        def _(k):
            ar_row(e, k).wait_send()

    @pl.loop(0, 4)
    def _(j):
        core_copy(j).wait_send()

    for step in range(3):
        for part in range(3):
            for k in (1, 2, 3):
                axis_copy(step, part, k).wait_send()


def body(marginal, penalty, ld_diag, ld_low, band, genotypes):
    place = lax.axis_index(("row", "col"))
    reach = jnp.arange(1, 3)
    mask = jnp.logical_and(band[0] >= reach, place >= reach).astype(F32)
    vmem = pl.BlockSpec(memory_space=pltpu.VMEM)
    smem = pl.BlockSpec(memory_space=pltpu.SMEM)
    hbm = pl.BlockSpec(memory_space=pl.ANY)
    big = lambda *lead: pltpu.VMEM((*lead, BS, K), F32)
    parts = []
    for _, size, order in PARTS:
        parts += [pltpu.VMEM((3, 4, 4, size, K), F32), pltpu.VMEM((3, 4, size, K), F32), pltpu.VMEM((3, size, K), F32)]
    dma = pltpu.SemaphoreType.DMA
    return pl.pallas_call(
        kernel,
        out_shape=(jax.ShapeDtypeStruct((BS, K), F32), jax.ShapeDtypeStruct((40, K), F32)),
        in_specs=[smem, vmem, vmem, hbm, hbm, hbm],
        out_specs=(vmem, vmem),
        scratch_shapes=[
            pltpu.VMEM((2, HALF, BS), F32),
            pltpu.VMEM((3, 2, BS, BS), BF16),
            pltpu.VMEM((2, 2, BS, BS), BF16),
            pltpu.VMEM((8 * GROUP, BS), BF16),
            big(2), big(3), big(3),
            pltpu.VMEM((BS, 2 * K), BF16),
            big(2), big(2), big(2), big(2), big(3), big(),
            big(), big(), big(), big(), big(),
            pltpu.VMEM((BS, K), BF16),
            pltpu.VMEM((3, 8, K), F32),
            pltpu.VMEM((3, COLS, 8, K), F32),
            pltpu.VMEM((3, ROWS, 8, K), F32),
            pltpu.VMEM((3, 8, K), F32),
            pltpu.VMEM((4, 4, 4, 40, K), F32),
            pltpu.VMEM((4, 4, 4, 40, K), F32),
            pltpu.VMEM((4, 4, 4, 40, K), F32),
            *parts,
            *[pltpu.VMEM((4, 4, size, K), F32) for _, size, _ in PARTS],
            *[pltpu.VMEM((4, size, K), F32) for _, size, _ in PARTS],
            dma((2,)), dma,
            dma((3, 4, NC)), dma((3, 4, NC)),
            dma((3, 2, COLS)), dma((3, 2, COLS)),
            dma((4,)), dma((4,)),
            dma((3, 3, 4)), dma((3, 3, 4)),
        ],
        compiler_params=pltpu.CompilerParams(
            collective_id=0, has_side_effects=True, vmem_limit_bytes=62 * 1024 * 1024
        ),
    )(mask, marginal, penalty.reshape(1, K), ld_diag, ld_low, genotypes)


def solution(mesh):
    placed = (
        P(("row", "col"), None),
        P(),
        P(("row", "col"), None, None),
        P(("row", "col"), None, None, None),
        P(("row", "col")),
        P(None, ("row", "col")),
    )
    return jax.shard_map(
        body,
        mesh=mesh,
        in_specs=placed,
        out_specs=(P(("row", "col"), None), P(("row", "col"), None)),
        check_vma=False,
    )
```

```python
import jax
import jax.numpy as jnp
from jax import lax
from jax.experimental import pallas as pl
from jax.experimental.pallas import tpu as pltpu
from jax.sharding import PartitionSpec as P

MESH = pl.DeviceIdType.MESH
F32 = jnp.float32
BF16 = jnp.bfloat16
BS = 1024
K = 128
ROWS = 8
COLS = 16
CH = 256
NC = BS // CH
GROUP = 640
PARTS = ((0, 16, "yzx"), (16, 16, "zxy"), (32, 8, "xyz"))


def split(v):
    high = v.astype(BF16)
    return high, (v - high.astype(F32)).astype(BF16)


def both(v):
    return jnp.concatenate(split(v), axis=1)


def dot(a, b):
    return jnp.dot(a, b, preferred_element_type=F32)


def product(high, low, pair):
    wide = dot(high, pair)
    return wide[:, :K] + wide[:, K:] + dot(low, pair[:, :K])


def chunk(c):
    return pl.ds(pl.multiple_of(c * CH, CH), CH)


def kernel(
    band, marginal, penalty_in, ld_diag, ld_low, genotypes,
    effects, scores,
    stage, diag_stage, tiles, flipped, geno, vec, m1, m2, via, pair, tail, u2, ru2, us, rus, look, dw,
    penalty, q1, r1, d1, d2, x01, rounded, payload, ar_one, ar_two, mid,
    sc, rc, total, p0a, p0b, p0c, p1a, p1b, p1c, p2a, p2b, p2c, v0, v1, v2, w0, w1, w2, mine40,
    small_sem, load_sem, diag_sem, geno_sem, out_sem, chain_s, chain_r, ar_s, ar_r, core_s, core_r,
    rs_s, rs_r, first_s, first_r,
):
    row, col = lax.axis_index("row"), lax.axis_index("col")
    place = row * COLS + col
    y, core, x, z = row // 2, row % 2, col // 4, col % 4

    def hop(distance):
        to = (place + distance + ROWS * COLS) % (ROWS * COLS)
        return (to // COLS, to % COLS)

    def at(**new):
        p = dict(y=y, core=core, x=x, z=z)
        p.update(new)
        return (p["y"] * 2 + p["core"], p["x"] * 4 + p["z"])

    back = at(z=(z + 3) % 4)
    onward = hop(jnp.where(z == 3, -1, 3))
    from_onward = hop(jnp.where(z == 2, 1, -3))

    b_copy = pltpu.make_async_copy(marginal, vec.at[0], small_sem.at[0])
    penalty_copy = pltpu.make_async_copy(penalty_in, penalty, small_sem.at[1])
    geno_copy = pltpu.make_async_copy(genotypes, geno, geno_sem)

    def load(t, c):
        return pltpu.make_async_copy(ld_low.at[0, 1 - t, :, chunk(c)], stage.at[c], load_sem.at[c])

    def load_diag(c):
        return pltpu.make_async_copy(ld_diag.at[0, chunk(c)], diag_stage.at[c], diag_sem.at[c])

    b_copy.start()
    penalty_copy.start()
    for c in range(NC):
        load(0, c).start()

    barrier = pltpu.get_barrier_semaphore()
    for device in (hop(1), hop(2), hop(-1), hop(-2), onward, from_onward):
        pl.semaphore_signal(barrier, inc=1, device_id=device, device_id_type=MESH)

    @pl.loop(1, COLS)
    def _(k):
        pl.semaphore_signal(barrier, inc=1, device_id=(row, (col + k) % COLS), device_id_type=MESH)

    @pl.loop(1, ROWS)
    def _(k):
        pl.semaphore_signal(barrier, inc=1, device_id=((row + k) % ROWS, col), device_id_type=MESH)

    b_copy.wait()
    pl.semaphore_wait(barrier, 6 + COLS - 1 + ROWS - 1)

    def remote(src, dst, send, recv, device):
        return pltpu.make_async_remote_copy(
            src_ref=src, dst_ref=dst, send_sem=send, recv_sem=recv,
            device_id=device, device_id_type=MESH,
        )

    def send_own(e, c):
        return remote(vec.at[e, chunk(c)], m1.at[e, chunk(c)],
                      chain_s.at[e, 0, c], chain_r.at[e, 0, c], hop(1))

    def send_on(e, c):
        return remote(m1.at[e, chunk(c)], m2.at[e, chunk(c)],
                      chain_s.at[e, 1, c], chain_r.at[e, 1, c], hop(1))

    def send_u2(e, c):
        return remote(u2.at[e, chunk(c)], ru2.at[e, chunk(c)],
                      chain_s.at[e, 2, c], chain_r.at[e, 2, c], hop(-1))

    def send_us(e, c):
        return remote(us.at[e, chunk(c)], rus.at[e, chunk(c)],
                      chain_s.at[e, 3, c], chain_r.at[e, 3, c], hop(-1))

    def send_back(c):
        return remote(vec.at[2, chunk(c)], via.at[chunk(c)],
                      chain_s.at[2, 2, c], chain_r.at[2, 2, c], back)

    def send_onward(c):
        return remote(via.at[chunk(c)], m2.at[2, chunk(c)],
                      chain_s.at[2, 3, c], chain_r.at[2, 3, c], onward)

    @pl.loop(0, NC)
    def _(c):
        send_own(0, c).start()

    for c in range(NC):
        load_diag(c).start()

    place_f = [place >= distance for distance in (1, 2)]
    active = [
        jnp.where(jnp.logical_and(place_f[d - 1], band[0] >= d), 1.0, 0.0).astype(F32) for d in (1, 2)
    ]

    def convert(t, c):
        load(t, c).wait()
        block = stage[c] * active[1 - t]
        high, low = split(block)
        tiles[t, 0, :, chunk(c)] = high
        tiles[t, 1, :, chunk(c)] = low
        high, low = split(block.T)
        flipped[t, 0, chunk(c), :] = high
        flipped[t, 1, chunk(c), :] = low
        if t == 0:
            load(1, c).start()

    def ar_col(n, k):
        return remote(payload.at[n], ar_one.at[n, k], ar_s.at[n, 0, k], ar_r.at[n, 0, k],
                      (row, (col + k) % COLS))

    def ar_row(n, k):
        return remote(mid.at[n], ar_two.at[n, k], ar_s.at[n, 1, k], ar_r.at[n, 1, k],
                      ((row + k) % ROWS, col))

    def ar_start(n, rows):
        for j in range(8):
            payload[n, j : j + 1, :] = rows[j] if j < len(rows) else jnp.zeros((1, K), F32)

        @pl.loop(1, COLS)
        def _(k):
            ar_col(n, k).start()

    def ar_middle(n):
        @pl.loop(1, COLS)
        def _(k):
            ar_col(n, k).wait_recv()

        acc = payload[n]
        for k in range(1, COLS):
            acc = acc + ar_one[n, k]
        mid[n] = acc

        @pl.loop(1, ROWS)
        def _(k):
            ar_row(n, k).start()

    def ar_end(n):
        @pl.loop(1, ROWS)
        def _(k):
            ar_row(n, k).wait_recv()

        acc = mid[n]
        for k in range(1, ROWS):
            acc = acc + ar_two[n, k]
        return acc

    def column(v):
        return jnp.sum(v, axis=0, keepdims=True)

    def over_chunks(body, count):
        zero = jnp.zeros((1, K), F32)
        return lax.fori_loop(0, NC, body, (zero,) * count)

    def add_second(e, c):
        there = both(m2[e, chunk(c), :])
        for r in range(NC):
            rows = pl.ds(r * CH, CH)
            look[e, rows, :] += product(tiles[0, 0, rows, chunk(c)], tiles[0, 1, rows, chunk(c)], there)

    def add_first(e, c):
        there = both(m1[e, chunk(c), :])
        for r in range(NC):
            rows = pl.ds(r * CH, CH)
            part = product(tiles[1, 0, rows, chunk(c)], tiles[1, 1, rows, chunk(c)], there)
            look[e, rows, :] = jnp.where(c == 0, part, part + look[e, rows, :])

    def below(e, r, last):
        return look[e, chunk(r), :] + product(
            tiles[0, 0, chunk(r), chunk(last)], tiles[0, 1, chunk(r), chunk(last)], tail[...]
        )

    def diagonal(e):
        @pl.loop(0, NC)
        def _(c):
            if e == 0:
                load_diag(c).wait()
                high, low = split(diag_stage[c])
                tiles[2, 0, chunk(c), :] = high
                tiles[2, 1, chunk(c), :] = low
            dw[chunk(c), :] = (
                product(tiles[2, 0, chunk(c), :], tiles[2, 1, chunk(c), :], pair[...])
                + penalty[...] * vec[e, chunk(c), :]
            )

    def exchange(e, early, middle, late):
        @pl.loop(0, NC)
        def _(c):
            if e == 0:
                convert(0, c)
            u2[e, chunk(c), :] = product(flipped[0, 0, chunk(c), :], flipped[0, 1, chunk(c), :], pair[...])
            send_u2(e, c).start()

        early()

        @pl.loop(0, NC)
        def _(c):
            send_own(e, c).wait_recv()
            send_on(e, c).start()
            if e == 0:
                convert(1, c)
            up = product(flipped[1, 0, chunk(c), :], flipped[1, 1, chunk(c), :], pair[...])
            send_u2(e, c).wait_recv()
            us[e, chunk(c), :] = up + ru2[e, chunk(c), :]
            send_us(e, c).start()
            add_first(e, c)

        middle()
        diagonal(e)
        late()

        @pl.loop(0, NC - 1)
        def _(c):
            send_on(e, c).wait_recv()
            add_second(e, c)

        send_on(e, NC - 1).wait_recv()
        tail[...] = both(m2[e, chunk(NC - 1), :])

    def finish(e, c):
        down = below(e, c, NC - 1)
        part = dw[chunk(c), :]
        send_us(e, c).wait_recv()
        out = part + down + rus[e, chunk(c), :]
        vec[e + 1, chunk(c), :] = out
        send_own(e + 1, c).start()
        look[e, chunk(c), :] = part + 2.0 * down
        pair[chunk(c), :] = both(out)
        return out

    @pl.loop(0, NC)
    def _(c):
        pair[chunk(c), :] = both(vec[0, chunk(c), :])

    penalty_copy.wait()
    exchange(0, lambda: None, geno_copy.start, lambda: None)

    def one(c, sums):
        out = finish(0, c)
        here = vec[0, chunk(c), :]
        return (sums[0] + column(here * here), sums[1] + column(here * out), sums[2] + column(out * out))

    sums_one = over_chunks(one, 3)

    coef = {}

    def late_one():
        got = ar_end(0)
        bb, bq, qq = got[0:1], got[1:2], got[2:3]
        alpha = bb / bq
        after = jnp.maximum(bb - 2.0 * alpha * bq + alpha * alpha * qq, 0.0)
        coef["a0"], coef["b1"] = alpha, after / bb

    exchange(1, lambda: ar_start(0, sums_one), lambda: ar_middle(0), late_one)
    a0, b1 = coef["a0"], coef["b1"]

    def two(c, sums):
        s = finish(1, c)
        here, q = vec[0, chunk(c), :], vec[1, chunk(c), :]
        res = here - a0 * q
        direction = res + b1 * here
        image = (1.0 + b1) * q - a0 * s
        r1[chunk(c), :] = res
        d1[chunk(c), :] = direction
        q1[chunk(c), :] = image
        terms = (res * res, res * direction, direction * image, res * image, image * image)
        return tuple(t + column(v) for t, v in zip(sums, terms))

    sums_two = over_chunks(two, 5)
    for c in (2, 3):
        send_back(c).start()
    ar_start(1, sums_two)

    for c in range(NC):
        send_own(2, c).wait_recv()
        if c < 2:
            send_on(2, c).start()
        else:
            send_back(c).wait_recv()
            send_onward(c).start()
        add_first(2, c)
    ar_middle(1)
    diagonal(2)
    got = ar_end(1)
    rr, rd, dq, rq, qq = (got[j : j + 1] for j in range(5))
    a1 = rd / dq
    after = jnp.maximum(rr - 2.0 * a1 * rq + a1 * a1 * qq, 0.0)
    b2 = after / rr

    def update(c, sums):
        res = r1[chunk(c), :] - a1 * q1[chunk(c), :]
        direction = res + b2 * d1[chunk(c), :]
        d2[chunk(c), :] = direction
        x01[chunk(c), :] = a0 * vec[0, chunk(c), :] + a1 * d1[chunk(c), :]
        return (sums[0] + column(res * direction),)

    rd2 = over_chunks(update, 1)[0]
    c0 = 1.0 + b2 * (1.0 + b1)
    c1 = -a0 - a1 * (1.0 + b1) - b2 * a0
    c2 = a1 * a0

    for c in (2, 3):
        send_onward(c).wait_recv()
        add_second(2, c)
    send_on(2, 0).wait_recv()
    add_second(2, 0)
    send_on(2, 1).wait_recv()
    tail[...] = both(m2[2, chunk(1), :])

    def three(c, sums):
        third = dw[chunk(c), :] + 2.0 * below(2, c, 1)
        image = c0 * look[0, chunk(c), :] + c1 * look[1, chunk(c), :] + c2 * third
        return (sums[0] + column(d2[chunk(c), :] * image),)

    dq2 = over_chunks(three, 1)[0]
    ar_start(2, (rd2, dq2))
    geno_copy.wait()
    ar_middle(2)
    got = ar_end(2)
    a2 = got[0:1] / got[1:2]

    @pl.loop(0, NC)
    def _(c):
        value = x01[chunk(c), :] + a2 * d2[chunk(c), :]
        x01[chunk(c), :] = value
        rounded[chunk(c), :] = value.astype(BF16)

    effects_copy = pltpu.make_async_copy(x01, effects, out_sem.at[0])
    effects_copy.start()

    def people(j, which):
        rows = pl.ds(pl.multiple_of((j * 2 + which) * GROUP, GROUP), GROUP)
        return dot(geno[rows, :], rounded[...]).reshape(4, 4, 40, K)

    def core_copy(j):
        return remote(sc.at[j], rc.at[j], core_s.at[j], core_r.at[j], at(core=1 - core))

    def rows_of(part):
        return pl.ds(PARTS[part][0], PARTS[part][1])

    def first_y(k):
        to = (y + k) % 4
        return remote(total.at[to, :, :, rows_of(0), :], p0a.at[k - 1], rs_s.at[0, 0, k], rs_r.at[0, 0, k], at(y=to))

    def first_z(j, k):
        to = (z + k) % 4
        return remote(total.at[j, :, to, rows_of(1), :], p1a.at[k - 1, j], first_s.at[0, k, j], first_r.at[0, k, j], at(z=to))

    def first_x(j, k):
        to = (x + k) % 4
        return remote(total.at[j, to, :, rows_of(2), :], p2a.at[k - 1, j], first_s.at[1, k, j], first_r.at[1, k, j], at(x=to))

    def other_core(n):
        j = (y + n) % 4
        sc[j] = people(j, 1 - core)
        core_copy(j).start()

    def own_core(n):
        j = (y + n) % 4
        mine = people(j, core)
        core_copy(j).wait_recv()
        total[j] = mine + rc[j]
        if n > 0:
            first_y(n).start()
        for k in (1, 3, 2):
            first_z(j, k).start()
            first_x(j, k).start()

    other_core(1)
    other_core(3)
    own_core(1)
    other_core(2)
    own_core(3)
    other_core(0)
    own_core(2)
    own_core(0)

    landed = ((p0a, p0b, p0c), (p1a, p1b, p1c), (p2a, p2b, p2c))
    halfway = ((v0, w0), (v1, w1), (v2, w2))

    def axis_copy(step, part, k):
        order = PARTS[part][2]
        axis = order[step]
        to = (dict(y=y, x=x, z=z)[axis] + k) % 4
        ref = halfway[part][step - 1]
        left = [a for a in "yxz" if a != order[0]]
        src = ref.at[:, to] if step == 1 and left[1] == axis else ref.at[to]
        return remote(src, landed[part][step].at[k - 1], rs_s.at[step, part, k], rs_r.at[step, part, k], at(**{axis: to}))

    def send_axis(step, part):
        for k in (1, 3, 2):
            axis_copy(step, part, k).start()

    for part in (2, 0, 1):
        acc = (
            lambda: total[y, :, :, rows_of(0), :],
            lambda: total[:, :, z, rows_of(1), :],
            lambda: total[:, x, :, rows_of(2), :],
        )[part]()
        for k in (1, 3, 2):
            if part == 0:
                first_y(k).wait_recv()
            else:
                for n in (1, 3, 2, 0):
                    (first_z, first_x)[part - 1]((y + n) % 4, k).wait_recv()
            acc = acc + landed[part][0][k - 1]
        halfway[part][0][...] = acc
        send_axis(1, part)
    for step in (1, 2):
        for part in (2, 0, 1):
            order = PARTS[part][2]
            axis = order[step]
            mine = dict(y=y, x=x, z=z)[axis]
            ref = halfway[part][step - 1]
            left = [a for a in "yxz" if a != order[0]]
            acc = ref[:, mine] if step == 1 and left[1] == axis else ref[mine]
            for k in (1, 3, 2):
                axis_copy(step, part, k).wait_recv()
                acc = acc + landed[part][step][k - 1]
            if step == 1:
                halfway[part][1][...] = acc
                send_axis(2, part)
            else:
                mine40[rows_of(part), :] = acc

    scores_copy = pltpu.make_async_copy(mine40, scores, out_sem.at[1])
    scores_copy.start()

    for e in range(3):
        @pl.loop(0, NC)
        def _(c):
            send_own(e, c).wait_send()
            if e < 2:
                send_on(e, c).wait_send()
                send_u2(e, c).wait_send()
                send_us(e, c).wait_send()

        @pl.loop(1, COLS)
        def _(k):
            ar_col(e, k).wait_send()

        @pl.loop(1, ROWS)
        def _(k):
            ar_row(e, k).wait_send()

    for c in (0, 1):
        send_on(2, c).wait_send()
    for c in (2, 3):
        send_back(c).wait_send()
        send_onward(c).wait_send()

    @pl.loop(0, 4)
    def _(j):
        core_copy(j).wait_send()

        @pl.loop(1, 4)
        def _(k):
            first_z(j, k).wait_send()
            first_x(j, k).wait_send()

    for k in (1, 2, 3):
        first_y(k).wait_send()
        for step in (1, 2):
            for part in range(3):
                axis_copy(step, part, k).wait_send()
    effects_copy.wait()
    scores_copy.wait()


def body(marginal, penalty, ld_diag, ld_low, band, genotypes):
    smem = pl.BlockSpec(memory_space=pltpu.SMEM)
    hbm = pl.BlockSpec(memory_space=pl.ANY)
    big = lambda *lead: pltpu.VMEM((*lead, BS, K), F32)
    parts = []
    for _, size, order in PARTS:
        parts += [pltpu.VMEM((3, 4, 4, size, K), F32), pltpu.VMEM((3, 4, size, K), F32), pltpu.VMEM((3, size, K), F32)]
    dma = pltpu.SemaphoreType.DMA
    return pl.pallas_call(
        kernel,
        out_shape=(jax.ShapeDtypeStruct((BS, K), F32), jax.ShapeDtypeStruct((40, K), F32)),
        in_specs=[smem, hbm, hbm, hbm, hbm, hbm],
        out_specs=(hbm, hbm),
        scratch_shapes=[
            pltpu.VMEM((NC, BS, CH), F32),
            pltpu.VMEM((NC, CH, BS), F32),
            pltpu.VMEM((3, 2, BS, BS), BF16),
            pltpu.VMEM((2, 2, BS, BS), BF16),
            pltpu.VMEM((8 * GROUP, BS), BF16),
            big(3), big(3), big(3), big(),
            pltpu.VMEM((BS, 2 * K), BF16),
            pltpu.VMEM((CH, 2 * K), BF16),
            big(2), big(2), big(2), big(2), big(3), big(),
            pltpu.VMEM((1, K), F32), big(), big(), big(), big(), big(),
            pltpu.VMEM((BS, K), BF16),
            pltpu.VMEM((3, 8, K), F32),
            pltpu.VMEM((3, COLS, 8, K), F32),
            pltpu.VMEM((3, ROWS, 8, K), F32),
            pltpu.VMEM((3, 8, K), F32),
            pltpu.VMEM((4, 4, 4, 40, K), F32),
            pltpu.VMEM((4, 4, 4, 40, K), F32),
            pltpu.VMEM((4, 4, 4, 40, K), F32),
            *parts,
            *[pltpu.VMEM((4, 4, size, K), F32) for _, size, _ in PARTS],
            *[pltpu.VMEM((4, size, K), F32) for _, size, _ in PARTS],
            pltpu.VMEM((40, K), F32),
            dma((2,)), dma((NC,)), dma((NC,)), dma, dma((2,)),
            dma((3, 4, NC)), dma((3, 4, NC)),
            dma((3, 2, COLS)), dma((3, 2, COLS)),
            dma((4,)), dma((4,)),
            dma((3, 3, 4)), dma((3, 3, 4)),
            dma((2, 4, 4)), dma((2, 4, 4)),
        ],
        compiler_params=pltpu.CompilerParams(
            collective_id=0, has_side_effects=True, vmem_limit_bytes=63 * 1024 * 1024
        ),
    )(band, marginal, penalty.reshape(1, K), ld_diag, ld_low, genotypes)


def solution(mesh):
    placed = (
        P(("row", "col"), None),
        P(),
        P(("row", "col"), None, None),
        P(("row", "col"), None, None, None),
        P(("row", "col")),
        P(None, ("row", "col")),
    )
    return jax.shard_map(
        body,
        mesh=mesh,
        in_specs=placed,
        out_specs=(P(("row", "col"), None), P(("row", "col"), None)),
        check_vma=False,
    )
```

```python
import jax
import jax.numpy as jnp
from jax import lax
from jax.experimental import pallas as pl
from jax.experimental.pallas import tpu as pltpu
from jax.sharding import PartitionSpec as P

MESH = pl.DeviceIdType.MESH
F32 = jnp.float32
BF16 = jnp.bfloat16
BS = 1024
K = 128
ROWS = 8
COLS = 16
CH = 256
NC = BS // CH
GROUP = 640
PARTS = ((0, 16, "yzx"), (16, 16, "zxy"), (32, 8, "xyz"))


def split(v):
    high = v.astype(BF16)
    return high, (v - high.astype(F32)).astype(BF16)


def both(v):
    return jnp.concatenate(split(v), axis=1)


def dot(a, b):
    return jnp.dot(a, b, preferred_element_type=F32)


def product(high, low, pair):
    wide = dot(high, pair)
    return wide[:, :K] + wide[:, K:] + dot(low, pair[:, :K])


def chunk(c):
    return pl.ds(pl.multiple_of(c * CH, CH), CH)


def kernel(
    band_in, marginal, penalty_in, ld_diag, ld_low, genotypes,
    effects, scores,
    band, stage, diag_stage, tiles, flipped, geno, vec, m1, m2, via, pair, tail, u2, ru2, us, rus, look, dw,
    penalty, q1, r1, d1, d2, x01, rounded, coef, payload, ar_one, ar_two, ar_three, mid_x, mid_y,
    sc, rc, total, p0a, p0b, p0c, p1a, p1b, p1c, p2a, p2b, p2c, v0, v1, v2, w0, w1, w2, mine40,
    small_sem, load_sem, diag_sem, geno_sem, out_sem, chain_s, chain_r, ar_s, ar_r, core_s, core_r,
    rs_s, rs_r, first_s, first_r,
):
    row, col = lax.axis_index("row"), lax.axis_index("col")
    place = row * COLS + col
    y, core, x, z = row // 2, row % 2, col // 4, col % 4

    def hop(distance):
        to = (place + distance + ROWS * COLS) % (ROWS * COLS)
        return (to // COLS, to % COLS)

    def at(**new):
        p = dict(y=y, core=core, x=x, z=z)
        p.update(new)
        return (p["y"] * 2 + p["core"], p["x"] * 4 + p["z"])

    back = at(z=(z + 3) % 4)
    onward = hop(jnp.where(z == 3, -1, 3))
    from_onward = hop(jnp.where(z == 2, 1, -3))

    b_copy = pltpu.make_async_copy(marginal, vec.at[0], small_sem.at[0])
    band_copy = pltpu.make_async_copy(band_in, band, small_sem.at[2])
    penalty_copy = pltpu.make_async_copy(penalty_in, penalty, small_sem.at[1])
    geno_copy = pltpu.make_async_copy(genotypes, geno, geno_sem)

    def load(t, c):
        return pltpu.make_async_copy(ld_low.at[0, 1 - t, :, chunk(c)], stage.at[c], load_sem.at[c])

    def load_diag(c):
        return pltpu.make_async_copy(ld_diag.at[0, chunk(c)], diag_stage.at[c], diag_sem.at[c])

    band_copy.start()
    b_copy.start()
    penalty_copy.start()
    for c in range(NC):
        load(0, c).start()

    barrier = pltpu.get_barrier_semaphore()
    for device in (hop(1), hop(2), hop(-1), hop(-2), onward, from_onward):
        pl.semaphore_signal(barrier, inc=1, device_id=device, device_id_type=MESH)

    straight = [at(z=(z + k % 4) % 4, core=(core + k // 4) % 2) for k in range(1, 8)]
    straight += [at(x=(x + k) % 4) for k in (1, 2, 3)] + [at(y=(y + k) % 4) for k in (1, 2, 3)]
    for device in straight:
        pl.semaphore_signal(barrier, inc=1, device_id=device, device_id_type=MESH)

    b_copy.wait()
    band_copy.wait()
    pl.semaphore_wait(barrier, 6 + len(straight))

    def remote(src, dst, send, recv, device):
        return pltpu.make_async_remote_copy(
            src_ref=src, dst_ref=dst, send_sem=send, recv_sem=recv,
            device_id=device, device_id_type=MESH,
        )

    def send_own(e, c):
        return remote(vec.at[e, chunk(c)], m1.at[e, chunk(c)],
                      chain_s.at[e, 0, c], chain_r.at[e, 0, c], hop(1))

    def send_on(e, c):
        return remote(m1.at[e, chunk(c)], m2.at[e, chunk(c)],
                      chain_s.at[e, 1, c], chain_r.at[e, 1, c], hop(1))

    def send_u2(e, c):
        return remote(u2.at[e, chunk(c)], ru2.at[e, chunk(c)],
                      chain_s.at[e, 2, c], chain_r.at[e, 2, c], hop(-1))

    def send_us(e, c):
        return remote(us.at[e, chunk(c)], rus.at[e, chunk(c)],
                      chain_s.at[e, 3, c], chain_r.at[e, 3, c], hop(-1))

    def send_back(c):
        return remote(vec.at[2, chunk(c)], via.at[chunk(c)],
                      chain_s.at[2, 2, c], chain_r.at[2, 2, c], back)

    def send_onward(c):
        return remote(via.at[chunk(c)], m2.at[2, chunk(c)],
                      chain_s.at[2, 3, c], chain_r.at[2, 3, c], onward)

    @pl.loop(0, NC)
    def _(c):
        send_own(0, c).start()

    for c in range(NC):
        load_diag(c).start()

    place_f = [place >= distance for distance in (1, 2)]
    active = [
        jnp.where(jnp.logical_and(place_f[d - 1], band[0] >= d), 1.0, 0.0).astype(F32) for d in (1, 2)
    ]

    def convert(t, c):
        load(t, c).wait()
        block = stage[c] * active[1 - t]
        high, low = split(block)
        tiles[t, 0, :, chunk(c)] = high
        tiles[t, 1, :, chunk(c)] = low
        high, low = split(block.T)
        flipped[t, 0, chunk(c), :] = high
        flipped[t, 1, chunk(c), :] = low
        if t == 0:
            load(1, c).start()

    def ar_copy(n, stage_no, k):
        src = (payload, mid_x, mid_y)[stage_no].at[n]
        if stage_no == 0:
            device = at(z=(z + k % 4) % 4, core=(core + k // 4) % 2)
        elif stage_no == 1:
            device = at(x=(x + k) % 4)
        else:
            device = at(y=(y + k) % 4)
        return remote(src, (ar_one, ar_two, ar_three)[stage_no].at[n, k],
                      ar_s.at[n, stage_no, k], ar_r.at[n, stage_no, k], device)

    def ar_send(n, stage_no):
        for k in range(1, (8, 4, 4)[stage_no]):
            ar_copy(n, stage_no, k).start()

    def ar_sum(n, stage_no):
        acc = (payload, mid_x, mid_y)[stage_no][n]
        for k in range(1, (8, 4, 4)[stage_no]):
            ar_copy(n, stage_no, k).wait_recv()
            acc = acc + (ar_one, ar_two, ar_three)[stage_no][n, k]
        return acc

    def ar_next(n, stage_no):
        (mid_x, mid_y)[stage_no][n] = ar_sum(n, stage_no)
        ar_send(n, stage_no + 1)

    def column(v):
        return jnp.sum(v, axis=0, keepdims=True)

    def over_chunks(n, body, count):
        zero = jnp.zeros((1, K), F32)
        sums = lax.fori_loop(0, NC, body, (zero,) * count)
        for j in range(count):
            payload[n, j : j + 1, :] = sums[j]

    def add_second(e, c):
        tail[...] = both(m2[e, chunk(c), :])

        @pl.loop(0, NC)
        def _(r):
            look[e, chunk(r), :] = below(e, r, c)

    def below(e, r, c):
        return look[e, chunk(r), :] + product(
            tiles[0, 0, chunk(r), chunk(c)], tiles[0, 1, chunk(r), chunk(c)], tail[...]
        )

    def add_first(e, c):
        tail[...] = both(m1[e, chunk(c), :])

        @pl.loop(0, NC)
        def _(r):
            part = product(tiles[1, 0, chunk(r), chunk(c)], tiles[1, 1, chunk(r), chunk(c)], tail[...])
            look[e, chunk(r), :] = jnp.where(c == 0, part, part + look[e, chunk(r), :])

    def diagonal(e):
        @pl.loop(0, NC)
        def _(c):
            @pl.when(e == 0)
            def _():
                load_diag(c).wait()
                high, low = split(diag_stage[c])
                tiles[2, 0, chunk(c), :] = high
                tiles[2, 1, chunk(c), :] = low

            dw[chunk(c), :] = (
                product(tiles[2, 0, chunk(c), :], tiles[2, 1, chunk(c), :], pair[...])
                + penalty[...] * vec[e, chunk(c), :]
            )

    def sums_one():
        def go(c, sums):
            here, out = vec[0, chunk(c), :], vec[1, chunk(c), :]
            return (sums[0] + column(here * here), sums[1] + column(here * out), sums[2] + column(out * out))

        over_chunks(0, go, 3)

    def solve_one():
        got = ar_sum(0, 2)
        bb, bq, qq = got[0:1], got[1:2], got[2:3]
        alpha = bb / bq
        after = jnp.maximum(bb - 2.0 * alpha * bq + alpha * alpha * qq, 0.0)
        coef[0:1, :] = alpha
        coef[1:2, :] = after / bb

    def sums_two():
        a0, b1 = coef[0:1, :], coef[1:2, :]

        def go(c, sums):
            here, q, s = vec[0, chunk(c), :], vec[1, chunk(c), :], vec[2, chunk(c), :]
            res = here - a0 * q
            direction = res + b1 * here
            image = (1.0 + b1) * q - a0 * s
            r1[chunk(c), :] = res
            d1[chunk(c), :] = direction
            q1[chunk(c), :] = image
            terms = (res * res, res * direction, direction * image, res * image, image * image)
            return tuple(t + column(v) for t, v in zip(sums, terms))

        over_chunks(1, go, 5)

    def solve_two():
        got = ar_sum(1, 2)
        rr, rd, dq, rq, qq = (got[j : j + 1] for j in range(5))
        a0 = coef[0:1, :]
        a1 = rd / dq
        after = jnp.maximum(rr - 2.0 * a1 * rq + a1 * a1 * qq, 0.0)
        b2 = after / rr
        coef[2:3, :] = a1
        coef[3:4, :] = b2

        @pl.loop(0, NC)
        def _(c):
            res = r1[chunk(c), :] - a1 * q1[chunk(c), :]
            r1[chunk(c), :] = res
            d2[chunk(c), :] = res + b2 * d1[chunk(c), :]
            x01[chunk(c), :] = a0 * vec[0, chunk(c), :] + a1 * d1[chunk(c), :]

    def sums_three():
        a0, b1, a1, b2 = (coef[j : j + 1, :] for j in range(4))
        c0 = 1.0 + b2 * (1.0 + b1)
        c1 = -a0 - a1 * (1.0 + b1) - b2 * a0
        c2 = a1 * a0

        def go(c, sums):
            direction = d2[chunk(c), :]
            image = c0 * look[0, chunk(c), :] + c1 * look[1, chunk(c), :] + c2 * look[2, chunk(c), :]
            return (sums[0] + column(r1[chunk(c), :] * direction), sums[1] + column(direction * image))

        over_chunks(2, go, 2)

    @pl.loop(0, NC)
    def _(c):
        pair[chunk(c), :] = both(vec[0, chunk(c), :])

    payload[...] = jnp.zeros_like(payload)
    penalty_copy.wait()

    @pl.loop(0, 3)
    def _(e):
        @pl.when(e == 2)
        def _():
            send_back(2).start()
            send_back(3).start()

        @pl.when(e < 2)
        def _():
            @pl.loop(0, NC)
            def _(c):
                @pl.when(e == 0)
                def _():
                    convert(0, c)

                u2[e, chunk(c), :] = product(flipped[0, 0, chunk(c), :], flipped[0, 1, chunk(c), :], pair[...])
                send_u2(e, c).start()

        @pl.when(e == 1)
        def _():
            sums_one()
            ar_send(0, 0)

        @pl.when(e == 2)
        def _():
            sums_two()
            ar_send(1, 0)

        @pl.loop(0, NC)
        def _(c):
            send_own(e, c).wait_recv()

            @pl.when(jnp.logical_or(e < 2, c < 2))
            def _():
                send_on(e, c).start()

            @pl.when(jnp.logical_and(e == 2, c >= 2))
            def _():
                send_back(c).wait_recv()
                send_onward(c).start()

            @pl.when(e == 0)
            def _():
                convert(1, c)

            @pl.when(e < 2)
            def _():
                up = product(flipped[1, 0, chunk(c), :], flipped[1, 1, chunk(c), :], pair[...])
                send_u2(e, c).wait_recv()
                us[e, chunk(c), :] = up + ru2[e, chunk(c), :]
                send_us(e, c).start()

            add_first(e, c)

        @pl.when(e == 0)
        def _():
            geno_copy.start()

        @pl.when(e > 0)
        def _():
            ar_next(e - 1, 0)

        diagonal(e)

        @pl.when(e > 0)
        def _():
            ar_next(e - 1, 1)

        def turn(i):
            return jnp.where(e == 2, (i + 2) % NC, i)

        def wait_second(c):
            @pl.when(jnp.logical_or(e < 2, c < 2))
            def _():
                send_on(e, c).wait_recv()

            @pl.when(jnp.logical_and(e == 2, c >= 2))
            def _():
                send_onward(c).wait_recv()

        @pl.loop(0, NC - 1)
        def _(i):
            wait_second(turn(i))
            add_second(e, turn(i))

        @pl.when(e == 1)
        def _():
            solve_one()

        @pl.when(e == 2)
        def _():
            solve_two()

        last = turn(NC - 1)
        wait_second(last)
        tail[...] = both(m2[e, chunk(last), :])

        @pl.loop(0, NC)
        def _(r):
            down = below(e, r, last)
            part = dw[chunk(r), :]
            look[e, chunk(r), :] = part + 2.0 * down

            @pl.when(e < 2)
            def _():
                send_us(e, r).wait_recv()
                out = part + down + rus[e, chunk(r), :]
                vec[e + 1, chunk(r), :] = out
                send_own(e + 1, r).start()
                pair[chunk(r), :] = both(out)

    sums_three()
    ar_send(2, 0)
    geno_copy.wait()
    ar_next(2, 0)
    ar_next(2, 1)
    got = ar_sum(2, 2)
    a2 = got[0:1] / got[1:2]

    @pl.loop(0, NC)
    def _(c):
        value = x01[chunk(c), :] + a2 * d2[chunk(c), :]
        x01[chunk(c), :] = value
        rounded[chunk(c), :] = value.astype(BF16)

    effects_copy = pltpu.make_async_copy(x01, effects, out_sem.at[0])
    effects_copy.start()

    def people(j, which):
        rows = pl.ds(pl.multiple_of((j * 2 + which) * GROUP, GROUP), GROUP)
        return dot(geno[rows, :], rounded[...]).reshape(4, 4, 40, K)

    def core_copy(j):
        return remote(sc.at[j], rc.at[j], core_s.at[j], core_r.at[j], at(core=1 - core))

    def rows_of(part):
        return pl.ds(PARTS[part][0], PARTS[part][1])

    def first_y(k):
        to = (y + k) % 4
        return remote(total.at[to, :, :, rows_of(0), :], p0a.at[k - 1], rs_s.at[0, 0, k], rs_r.at[0, 0, k], at(y=to))

    def first_z(j, k):
        to = (z + k) % 4
        return remote(total.at[j, :, to, rows_of(1), :], p1a.at[k - 1, j], first_s.at[0, k, j], first_r.at[0, k, j], at(z=to))

    def first_x(j, k):
        to = (x + k) % 4
        return remote(total.at[j, to, :, rows_of(2), :], p2a.at[k - 1, j], first_s.at[1, k, j], first_r.at[1, k, j], at(x=to))

    def other_core(n):
        j = (y + n) % 4
        sc[j] = people(j, 1 - core)
        core_copy(j).start()

    def own_core(n):
        j = (y + n) % 4
        mine = people(j, core)
        core_copy(j).wait_recv()
        total[j] = mine + rc[j]
        @pl.when(n > 0)
        def _():
            first_y(n).start()

        for k in (1, 3, 2):
            first_z(j, k).start()
            first_x(j, k).start()

    @pl.loop(0, 5)
    def _(i):
        @pl.when(i < 4)
        def _():
            other_core((i + 1) % 4)

        @pl.when(i > 0)
        def _():
            own_core(i % 4)

    landed = ((p0a, p0b, p0c), (p1a, p1b, p1c), (p2a, p2b, p2c))
    halfway = ((v0, w0), (v1, w1), (v2, w2))

    def axis_copy(step, part, k):
        order = PARTS[part][2]
        axis = order[step]
        to = (dict(y=y, x=x, z=z)[axis] + k) % 4
        ref = halfway[part][step - 1]
        left = [a for a in "yxz" if a != order[0]]
        src = ref.at[:, to] if step == 1 and left[1] == axis else ref.at[to]
        return remote(src, landed[part][step].at[k - 1], rs_s.at[step, part, k], rs_r.at[step, part, k], at(**{axis: to}))

    def send_axis(step, part):
        for k in (1, 3, 2):
            axis_copy(step, part, k).start()

    for part in (2, 0, 1):
        for k in (1, 3, 2):
            if part == 0:
                first_y(k).wait_recv()
            else:
                for n in (1, 2, 3, 0):
                    (first_z, first_x)[part - 1]((y + n) % 4, k).wait_recv()

        @pl.loop(0, 4)
        def _(i):
            acc = (
                lambda: total[y, i, :, rows_of(0), :],
                lambda: total[i, :, z, rows_of(1), :],
                lambda: total[i, x, :, rows_of(2), :],
            )[part]()
            for k in (1, 3, 2):
                acc = acc + landed[part][0][k - 1, i]
            halfway[part][0][i] = acc

        send_axis(1, part)
    for step in (1, 2):
        for part in (2, 0, 1):
            order = PARTS[part][2]
            axis = order[step]
            mine = dict(y=y, x=x, z=z)[axis]
            ref = halfway[part][step - 1]
            left = [a for a in "yxz" if a != order[0]]
            acc = ref[:, mine] if step == 1 and left[1] == axis else ref[mine]
            for k in (1, 3, 2):
                axis_copy(step, part, k).wait_recv()
                acc = acc + landed[part][step][k - 1]
            if step == 1:
                halfway[part][1][...] = acc
                send_axis(2, part)
            else:
                mine40[rows_of(part), :] = acc

    scores_copy = pltpu.make_async_copy(mine40, scores, out_sem.at[1])
    scores_copy.start()

    for e in range(3):
        @pl.loop(0, NC)
        def _(c):
            send_own(e, c).wait_send()
            if e < 2:
                send_on(e, c).wait_send()
                send_u2(e, c).wait_send()
                send_us(e, c).wait_send()

        for stage_no in range(3):
            for k in range(1, (8, 4, 4)[stage_no]):
                ar_copy(e, stage_no, k).wait_send()

    for c in (0, 1):
        send_on(2, c).wait_send()
    for c in (2, 3):
        send_back(c).wait_send()
        send_onward(c).wait_send()

    @pl.loop(0, 4)
    def _(j):
        core_copy(j).wait_send()

        @pl.loop(1, 4)
        def _(k):
            first_z(j, k).wait_send()
            first_x(j, k).wait_send()

    for k in (1, 2, 3):
        first_y(k).wait_send()
        for step in (1, 2):
            for part in range(3):
                axis_copy(step, part, k).wait_send()
    effects_copy.wait()
    scores_copy.wait()


def body(marginal, penalty, ld_diag, ld_low, band, genotypes):
    hbm = pl.BlockSpec(memory_space=pl.ANY)
    big = lambda *lead: pltpu.VMEM((*lead, BS, K), F32)
    parts = []
    for _, size, order in PARTS:
        parts += [pltpu.VMEM((3, 4, 4, size, K), F32), pltpu.VMEM((3, 4, size, K), F32), pltpu.VMEM((3, size, K), F32)]
    dma = pltpu.SemaphoreType.DMA
    return pl.pallas_call(
        kernel,
        out_shape=(jax.ShapeDtypeStruct((BS, K), F32), jax.ShapeDtypeStruct((40, K), F32)),
        in_specs=[hbm, hbm, hbm, hbm, hbm, hbm],
        out_specs=(hbm, hbm),
        scratch_shapes=[
            pltpu.SMEM((1,), jnp.int32),
            pltpu.VMEM((NC, BS, CH), F32),
            pltpu.VMEM((NC, CH, BS), F32),
            pltpu.VMEM((3, 2, BS, BS), BF16),
            pltpu.VMEM((2, 2, BS, BS), BF16),
            pltpu.VMEM((8 * GROUP, BS), BF16),
            big(3), big(3), big(3), big(),
            pltpu.VMEM((BS, 2 * K), BF16),
            pltpu.VMEM((CH, 2 * K), BF16),
            big(2), big(2), big(2), big(2), big(3), big(),
            pltpu.VMEM((1, K), F32), big(), big(), big(), big(), big(),
            pltpu.VMEM((BS, K), BF16),
            pltpu.VMEM((8, K), F32),
            pltpu.VMEM((3, 8, K), F32),
            pltpu.VMEM((3, 8, 8, K), F32),
            pltpu.VMEM((3, 4, 8, K), F32),
            pltpu.VMEM((3, 4, 8, K), F32),
            pltpu.VMEM((3, 8, K), F32),
            pltpu.VMEM((3, 8, K), F32),
            pltpu.VMEM((4, 4, 4, 40, K), F32),
            pltpu.VMEM((4, 4, 4, 40, K), F32),
            pltpu.VMEM((4, 4, 4, 40, K), F32),
            *parts,
            *[pltpu.VMEM((4, 4, size, K), F32) for _, size, _ in PARTS],
            *[pltpu.VMEM((4, size, K), F32) for _, size, _ in PARTS],
            pltpu.VMEM((40, K), F32),
            dma((3,)), dma((NC,)), dma((NC,)), dma, dma((2,)),
            dma((3, 4, NC)), dma((3, 4, NC)),
            dma((3, 3, 8)), dma((3, 3, 8)),
            dma((4,)), dma((4,)),
            dma((3, 3, 4)), dma((3, 3, 4)),
            dma((2, 4, 4)), dma((2, 4, 4)),
        ],
        compiler_params=pltpu.CompilerParams(
            collective_id=0, has_side_effects=True, vmem_limit_bytes=63 * 1024 * 1024
        ),
    )(band, marginal, penalty.reshape(1, K), ld_diag, ld_low, genotypes)


def solution(mesh):
    placed = (
        P(("row", "col"), None),
        P(),
        P(("row", "col"), None, None),
        P(("row", "col"), None, None, None),
        P(("row", "col")),
        P(None, ("row", "col")),
    )
    return jax.shard_map(
        body,
        mesh=mesh,
        in_specs=placed,
        out_specs=(P(("row", "col"), None), P(("row", "col"), None)),
        check_vma=False,
    )
```

```python
import jax
import jax.numpy as jnp
from jax import lax
from jax.experimental import pallas as pl
from jax.experimental.pallas import tpu as pltpu
from jax.sharding import PartitionSpec as P

MESH = pl.DeviceIdType.MESH
F32 = jnp.float32
BF16 = jnp.bfloat16
BS = 1024
K = 128
ROWS = 8
COLS = 16
CH = 256
NC = BS // CH
GROUP = 640
PARTS = ((0, 16, "yzx"), (16, 16, "zxy"), (32, 8, "xyz"))


def split(v):
    high = v.astype(BF16)
    return high, (v - high.astype(F32)).astype(BF16)


def both(v):
    return jnp.concatenate(split(v), axis=1)


def dot(a, b):
    return jnp.dot(a, b, preferred_element_type=F32)


def product(high, low, pair):
    wide = dot(high, pair)
    return wide[:, :K] + wide[:, K:] + dot(low, pair[:, :K])


def chunk(c):
    return pl.ds(pl.multiple_of(c * CH, CH), CH)


def kernel(
    band_in, marginal, penalty_in, ld_diag, ld_low, genotypes,
    effects, scores,
    band, stage, diag_stage, tiles, flipped, geno, vec, m1, m2, via, pair, tail, u2, ru2, us, rus, look, dw,
    penalty, q1, r1, d1, d2, x01, rounded, payload, ar_one, ar_two, mid,
    sc, rc, total, p0a, p0b, p0c, p1a, p1b, p1c, p2a, p2b, p2c, v0, v1, v2, w0, w1, w2, mine40,
    small_sem, load_sem, diag_sem, geno_sem, out_sem, chain_s, chain_r, up_r, via_r, ar_s, ar_r, core_s, core_r,
    rs_s, rs_r,
):
    row, col = lax.axis_index("row"), lax.axis_index("col")
    place = row * COLS + col
    y, core, x, z = row // 2, row % 2, col // 4, col % 4

    def hop(distance):
        to = (place + distance + ROWS * COLS) % (ROWS * COLS)
        return (to // COLS, to % COLS)

    def at(**new):
        p = dict(y=y, core=core, x=x, z=z)
        p.update(new)
        return (p["y"] * 2 + p["core"], p["x"] * 4 + p["z"])

    back = at(z=(z + 3) % 4)
    onward = hop(jnp.where(z == 3, -1, 3))
    from_onward = hop(jnp.where(z == 2, 1, -3))

    b_copy = pltpu.make_async_copy(marginal, vec.at[0], small_sem.at[0])
    band_copy = pltpu.make_async_copy(band_in, band, small_sem.at[2])
    penalty_copy = pltpu.make_async_copy(penalty_in, penalty, small_sem.at[1])
    geno_copy = pltpu.make_async_copy(genotypes, geno, geno_sem)

    def load(t, c):
        return pltpu.make_async_copy(ld_low.at[0, 1 - t, :, chunk(c)], stage.at[c], load_sem.at[c])

    def load_diag(c):
        return pltpu.make_async_copy(ld_diag.at[0, chunk(c)], diag_stage.at[c], diag_sem.at[c])

    band_copy.start()
    b_copy.start()
    penalty_copy.start()
    for c in range(NC):
        load(0, c).start()

    barrier = pltpu.get_barrier_semaphore()
    for device in (hop(1), hop(2), hop(-1), hop(-2), onward, from_onward):
        pl.semaphore_signal(barrier, inc=1, device_id=device, device_id_type=MESH)

    @pl.loop(1, COLS)
    def _(k):
        pl.semaphore_signal(barrier, inc=1, device_id=(row, (col + k) % COLS), device_id_type=MESH)

    @pl.loop(1, ROWS)
    def _(k):
        pl.semaphore_signal(barrier, inc=1, device_id=((row + k) % ROWS, col), device_id_type=MESH)

    b_copy.wait()
    band_copy.wait()
    pl.semaphore_wait(barrier, 6 + COLS - 1 + ROWS - 1)

    def remote(src, dst, send, recv, device):
        return pltpu.make_async_remote_copy(
            src_ref=src, dst_ref=dst, send_sem=send, recv_sem=recv,
            device_id=device, device_id_type=MESH,
        )

    def send_own(e, c):
        return remote(vec.at[e, chunk(c)], m1.at[e, chunk(c)],
                      chain_s.at[0], chain_r.at[e, 0, c], hop(1))

    def send_on(e, c):
        return remote(m1.at[e, chunk(c)], m2.at[e, chunk(c)],
                      chain_s.at[1 if e < 2 else 2], chain_r.at[e, 1, c], hop(1))

    def send_u2(e, c):
        return remote(u2.at[e, chunk(c)], ru2.at[e, chunk(c)],
                      chain_s.at[3], up_r.at[e, 0, c], hop(-1))

    def send_us(e, c):
        return remote(us.at[e, chunk(c)], rus.at[e, chunk(c)],
                      chain_s.at[4], up_r.at[e, 1, c], hop(-1))

    def send_back(c):
        return remote(vec.at[2, chunk(c)], via.at[chunk(c)],
                      chain_s.at[5], via_r.at[c - 2], back)

    def send_onward(c):
        return remote(via.at[chunk(c)], m2.at[2, chunk(c)],
                      chain_s.at[6], chain_r.at[2, 1, c], onward)

    @pl.loop(0, NC)
    def _(c):
        send_own(0, c).start()

    for c in range(NC):
        load_diag(c).start()

    place_f = [place >= distance for distance in (1, 2)]
    active = [
        jnp.where(jnp.logical_and(place_f[d - 1], band[0] >= d), 1.0, 0.0).astype(F32) for d in (1, 2)
    ]

    def convert(t, c):
        load(t, c).wait()
        block = stage[c] * active[1 - t]
        high, low = split(block)
        tiles[t, 0, :, chunk(c)] = high
        tiles[t, 1, :, chunk(c)] = low
        high, low = split(block.T)
        flipped[t, 0, chunk(c), :] = high
        flipped[t, 1, chunk(c), :] = low
        if t == 0:
            load(1, c).start()

    def ar_copy(n, step, k):
        if step == 0:
            return remote(payload.at[n], ar_one.at[n, k - 1], ar_s.at[0], ar_r.at[n, 0], (row, (col + k) % COLS))
        return remote(mid.at[n], ar_two.at[n, k - 1], ar_s.at[1], ar_r.at[n, 1], ((row + k) % ROWS, col))

    def ar_all(n, step):
        ref = (ar_one, ar_two)[step].at[n]
        return remote(ref, ref, ar_s.at[step], ar_r.at[n, step], hop(1))

    def ar_send(n, step):
        @pl.loop(1, (COLS, ROWS)[step])
        def _(k):
            ar_copy(n, step, k).start()

    def ar_start(n, rows):
        for j in range(8):
            payload[n, j : j + 1, :] = rows[j] if j < len(rows) else jnp.zeros((1, K), F32)
        ar_send(n, 0)

    def ar_sum(n, step):
        ar_all(n, step).wait_recv()
        acc = (payload, mid)[step][n]
        for k in range(1, (COLS, ROWS)[step]):
            acc = acc + (ar_one, ar_two)[step][n, k - 1]
        return acc

    def ar_next(n):
        mid[n] = ar_sum(n, 0)
        ar_send(n, 1)

    def column(v):
        return jnp.sum(v, axis=0, keepdims=True)

    def over_chunks(body, count):
        zero = jnp.zeros((1, K), F32)
        return lax.fori_loop(0, NC, body, (zero,) * count)

    def add_second(e, c):
        there = both(m2[e, chunk(c), :])
        for r in range(NC):
            rows = pl.ds(r * CH, CH)
            look[e, rows, :] += product(tiles[0, 0, rows, chunk(c)], tiles[0, 1, rows, chunk(c)], there)

    def add_first(e, c):
        there = both(m1[e, chunk(c), :])
        for r in range(NC):
            rows = pl.ds(r * CH, CH)
            part = product(tiles[1, 0, rows, chunk(c)], tiles[1, 1, rows, chunk(c)], there)
            look[e, rows, :] = jnp.where(c == 0, part, part + look[e, rows, :])

    def below(e, r, last):
        return look[e, chunk(r), :] + product(
            tiles[0, 0, chunk(r), chunk(last)], tiles[0, 1, chunk(r), chunk(last)], tail[...]
        )

    def diagonal(e):
        @pl.loop(0, NC)
        def _(c):
            if e == 0:
                load_diag(c).wait()
                high, low = split(diag_stage[c])
                tiles[2, 0, chunk(c), :] = high
                tiles[2, 1, chunk(c), :] = low
            dw[chunk(c), :] = (
                product(tiles[2, 0, chunk(c), :], tiles[2, 1, chunk(c), :], pair[...])
                + penalty[...] * vec[e, chunk(c), :]
            )

    def exchange(e, early, middle, between, late):
        @pl.loop(0, NC)
        def _(c):
            if e == 0:
                convert(0, c)
            u2[e, chunk(c), :] = product(flipped[0, 0, chunk(c), :], flipped[0, 1, chunk(c), :], pair[...])
            send_u2(e, c).start()

        early()

        @pl.loop(0, NC)
        def _(c):
            send_own(e, c).wait_recv()
            send_on(e, c).start()
            if e == 0:
                convert(1, c)
            up = product(flipped[1, 0, chunk(c), :], flipped[1, 1, chunk(c), :], pair[...])
            send_u2(e, c).wait_recv()
            us[e, chunk(c), :] = up + ru2[e, chunk(c), :]
            send_us(e, c).start()
            add_first(e, c)

        middle()
        diagonal(e)
        between()

        @pl.loop(0, NC - 1)
        def _(c):
            send_on(e, c).wait_recv()
            add_second(e, c)

        late()
        send_on(e, NC - 1).wait_recv()
        tail[...] = both(m2[e, chunk(NC - 1), :])

    def finish(e, c):
        down = below(e, c, NC - 1)
        part = dw[chunk(c), :]
        send_us(e, c).wait_recv()
        out = part + down + rus[e, chunk(c), :]
        vec[e + 1, chunk(c), :] = out
        send_own(e + 1, c).start()
        look[e, chunk(c), :] = part + 2.0 * down
        pair[chunk(c), :] = both(out)
        return out

    @pl.loop(0, NC)
    def _(c):
        pair[chunk(c), :] = both(vec[0, chunk(c), :])

    penalty_copy.wait()
    exchange(0, lambda: None, geno_copy.start, lambda: None, lambda: None)

    def one(c, sums):
        out = finish(0, c)
        here = vec[0, chunk(c), :]
        return (sums[0] + column(here * here), sums[1] + column(here * out), sums[2] + column(out * out))

    sums_one = over_chunks(one, 3)

    coef = {}

    def late_one():
        got = ar_sum(0, 1)
        bb, bq, qq = got[0:1], got[1:2], got[2:3]
        alpha = bb / bq
        after = jnp.maximum(bb - 2.0 * alpha * bq + alpha * alpha * qq, 0.0)
        coef["a0"], coef["b1"] = alpha, after / bb

    exchange(1, lambda: ar_start(0, sums_one), lambda: ar_next(0), lambda: None, lambda: None)

    @pl.loop(0, NC)
    def _(c):
        finish(1, c)

    for c in (2, 3):
        send_back(c).start()
    late_one()
    a0, b1 = coef["a0"], coef["b1"]

    def two(c, sums):
        here, q, s = vec[0, chunk(c), :], vec[1, chunk(c), :], vec[2, chunk(c), :]
        res = here - a0 * q
        direction = res + b1 * here
        image = (1.0 + b1) * q - a0 * s
        r1[chunk(c), :] = res
        d1[chunk(c), :] = direction
        q1[chunk(c), :] = image
        terms = (res * res, res * direction, direction * image, res * image, image * image)
        return tuple(t + column(v) for t, v in zip(sums, terms))

    sums_two = over_chunks(two, 5)
    ar_start(1, sums_two)

    for c in range(NC):
        send_own(2, c).wait_recv()
        if c < 2:
            send_on(2, c).start()
        else:
            send_back(c).wait_recv()
            send_onward(c).start()
        add_first(2, c)
    ar_next(1)
    diagonal(2)
    for c in (2, 3):
        send_onward(c).wait_recv()
        add_second(2, c)
    got = ar_sum(1, 1)
    rr, rd, dq, rq, qq = (got[j : j + 1] for j in range(5))
    a1 = rd / dq
    after = jnp.maximum(rr - 2.0 * a1 * rq + a1 * a1 * qq, 0.0)
    b2 = after / rr

    def update(c, sums):
        res = r1[chunk(c), :] - a1 * q1[chunk(c), :]
        direction = res + b2 * d1[chunk(c), :]
        d2[chunk(c), :] = direction
        x01[chunk(c), :] = a0 * vec[0, chunk(c), :] + a1 * d1[chunk(c), :]
        return (sums[0] + column(res * direction),)

    rd2 = over_chunks(update, 1)[0]
    c0 = 1.0 + b2 * (1.0 + b1)
    c1 = -a0 - a1 * (1.0 + b1) - b2 * a0
    c2 = a1 * a0

    send_on(2, 0).wait_recv()
    add_second(2, 0)
    send_on(2, 1).wait_recv()
    tail[...] = both(m2[2, chunk(1), :])

    def three(c, sums):
        third = dw[chunk(c), :] + 2.0 * below(2, c, 1)
        image = c0 * look[0, chunk(c), :] + c1 * look[1, chunk(c), :] + c2 * third
        return (sums[0] + column(d2[chunk(c), :] * image),)

    dq2 = over_chunks(three, 1)[0]
    ar_start(2, (rd2, dq2))
    geno_copy.wait()
    ar_next(2)
    got = ar_sum(2, 1)
    a2 = got[0:1] / got[1:2]

    @pl.loop(0, NC)
    def _(c):
        value = x01[chunk(c), :] + a2 * d2[chunk(c), :]
        x01[chunk(c), :] = value
        rounded[chunk(c), :] = value.astype(BF16)

    effects_copy = pltpu.make_async_copy(x01, effects, out_sem.at[0])
    effects_copy.start()

    def people(j, which):
        rows = pl.ds(pl.multiple_of((j * 2 + which) * GROUP, GROUP), GROUP)
        return dot(geno[rows, :], rounded[...]).reshape(4, 4, 40, K)

    def core_copy(j):
        return remote(sc.at[j], rc.at[j], core_s, core_r.at[j], at(core=1 - core))

    def rows_of(part):
        return pl.ds(PARTS[part][0], PARTS[part][1])

    def first_y(k):
        to = (y + k) % 4
        return remote(total.at[to, :, :, rows_of(0), :], p0a.at[k - 1], rs_s.at[0, 0], rs_r.at[0, 0], at(y=to))

    def first_z(j, k):
        to = (z + k) % 4
        return remote(total.at[j, :, to, rows_of(1), :], p1a.at[k - 1, j], rs_s.at[0, 1], rs_r.at[0, 1], at(z=to))

    def first_x(j, k):
        to = (x + k) % 4
        return remote(total.at[j, to, :, rows_of(2), :], p2a.at[k - 1, j], rs_s.at[0, 2], rs_r.at[0, 2], at(x=to))

    def other_core(n):
        j = (y + n) % 4
        sc[j] = people(j, 1 - core)
        core_copy(j).start()

    def own_core(n):
        j = (y + n) % 4
        mine = people(j, core)
        core_copy(j).wait_recv()
        total[j] = mine + rc[j]
        if n > 0:
            first_y(n).start()
        for k in (1, 3, 2):
            first_z(j, k).start()
            first_x(j, k).start()

    other_core(1)
    other_core(3)
    own_core(1)
    other_core(2)
    own_core(3)
    other_core(0)
    own_core(2)
    own_core(0)

    landed = ((p0a, p0b, p0c), (p1a, p1b, p1c), (p2a, p2b, p2c))
    halfway = ((v0, w0), (v1, w1), (v2, w2))

    def axis_copy(step, part, k):
        order = PARTS[part][2]
        axis = order[step]
        to = (dict(y=y, x=x, z=z)[axis] + k) % 4
        ref = halfway[part][step - 1]
        left = [a for a in "yxz" if a != order[0]]
        src = ref.at[:, to] if step == 1 and left[1] == axis else ref.at[to]
        return remote(src, landed[part][step].at[k - 1], rs_s.at[step, part], rs_r.at[step, part], at(**{axis: to}))

    def landing(step, part):
        ref = landed[part][step]
        return remote(ref, ref, rs_s.at[step, part], rs_r.at[step, part], hop(1))

    def send_axis(step, part):
        for k in (1, 3, 2):
            axis_copy(step, part, k).start()

    for part in (2, 0, 1):
        acc = (
            lambda: total[y, :, :, rows_of(0), :],
            lambda: total[:, :, z, rows_of(1), :],
            lambda: total[:, x, :, rows_of(2), :],
        )[part]()
        landing(0, part).wait_recv()
        for k in (1, 3, 2):
            acc = acc + landed[part][0][k - 1]
        halfway[part][0][...] = acc
        send_axis(1, part)
    for step in (1, 2):
        for part in (2, 0, 1):
            order = PARTS[part][2]
            axis = order[step]
            mine = dict(y=y, x=x, z=z)[axis]
            ref = halfway[part][step - 1]
            left = [a for a in "yxz" if a != order[0]]
            acc = ref[:, mine] if step == 1 and left[1] == axis else ref[mine]
            landing(step, part).wait_recv()
            for k in (1, 3, 2):
                acc = acc + landed[part][step][k - 1]
            if step == 1:
                halfway[part][1][...] = acc
                send_axis(2, part)
            else:
                mine40[rows_of(part), :] = acc

    scores_copy = pltpu.make_async_copy(mine40, scores, out_sem.at[1])
    scores_copy.start()

    def gone(ref, sem):
        remote(ref, ref, sem, sem, hop(1)).wait_send()

    gone(vec, chain_s.at[0])
    gone(m1.at[pl.ds(0, 2)], chain_s.at[1])
    gone(m1.at[2, pl.ds(0, 2 * CH)], chain_s.at[2])
    gone(u2, chain_s.at[3])
    gone(us, chain_s.at[4])
    gone(via.at[pl.ds(2 * CH, 2 * CH)], chain_s.at[5])
    gone(via.at[pl.ds(2 * CH, 2 * CH)], chain_s.at[6])
    for step, ref in enumerate((ar_one, ar_two)):
        gone(ref, ar_s.at[step])
    gone(sc, core_s)
    for step in range(3):
        for part in range(3):
            gone(landed[part][step], rs_s.at[step, part])
    effects_copy.wait()
    scores_copy.wait()


def copy_out(effects_in, scores_in, effects, scores):
    effects[...] = effects_in[...]
    scores[...] = scores_in[...]


def body(marginal, penalty, ld_diag, ld_low, band, genotypes):
    hbm = pl.BlockSpec(memory_space=pl.ANY)
    big = lambda *lead: pltpu.VMEM((*lead, BS, K), F32)
    parts = []
    for _, size, order in PARTS:
        parts += [pltpu.VMEM((3, 4, 4, size, K), F32), pltpu.VMEM((3, 4, size, K), F32), pltpu.VMEM((3, size, K), F32)]
    dma = pltpu.SemaphoreType.DMA
    shapes = (jax.ShapeDtypeStruct((BS, K), F32), jax.ShapeDtypeStruct((40, K), F32))
    results = pl.pallas_call(
        kernel,
        out_shape=shapes,
        in_specs=[hbm, hbm, hbm, hbm, hbm, hbm],
        out_specs=(hbm, hbm),
        scratch_shapes=[
            pltpu.SMEM((1,), jnp.int32),
            pltpu.VMEM((NC, BS, CH), F32),
            pltpu.VMEM((NC, CH, BS), F32),
            pltpu.VMEM((3, 2, BS, BS), BF16),
            pltpu.VMEM((2, 2, BS, BS), BF16),
            pltpu.VMEM((8 * GROUP, BS), BF16),
            big(3), big(3), big(3), big(),
            pltpu.VMEM((BS, 2 * K), BF16),
            pltpu.VMEM((CH, 2 * K), BF16),
            big(2), big(2), big(2), big(2), big(3), big(),
            pltpu.VMEM((1, K), F32), big(), big(), big(), big(), big(),
            pltpu.VMEM((BS, K), BF16),
            pltpu.VMEM((3, 8, K), F32),
            pltpu.VMEM((3, COLS - 1, 8, K), F32),
            pltpu.VMEM((3, ROWS - 1, 8, K), F32),
            pltpu.VMEM((3, 8, K), F32),
            pltpu.VMEM((4, 4, 4, 40, K), F32),
            pltpu.VMEM((4, 4, 4, 40, K), F32),
            pltpu.VMEM((4, 4, 4, 40, K), F32),
            *parts,
            *[pltpu.VMEM((4, 4, size, K), F32) for _, size, _ in PARTS],
            *[pltpu.VMEM((4, size, K), F32) for _, size, _ in PARTS],
            pltpu.VMEM((40, K), F32),
            dma((3,)), dma((NC,)), dma((NC,)), dma, dma((2,)),
            dma((7,)), dma((3, 2, NC)), dma((2, 2, NC)), dma((2,)),
            dma((2,)), dma((3, 2)),
            dma, dma((4,)),
            dma((3, 3)), dma((3, 3)),
        ],
        compiler_params=pltpu.CompilerParams(
            collective_id=0, has_side_effects=True, vmem_limit_bytes=63 * 1024 * 1024
        ),
    )(band, marginal, penalty.reshape(1, K), ld_diag, ld_low, genotypes)
    return pl.pallas_call(
        copy_out,
        out_shape=shapes,
    )(*results)


def solution(mesh):
    placed = (
        P(("row", "col"), None),
        P(),
        P(("row", "col"), None, None),
        P(("row", "col"), None, None, None),
        P(("row", "col")),
        P(None, ("row", "col")),
    )
    return jax.shard_map(
        body,
        mesh=mesh,
        in_specs=placed,
        out_specs=(P(("row", "col"), None), P(("row", "col"), None)),
        check_vma=False,
    )
```

```python
import jax
import jax.numpy as jnp
from jax import lax
from jax.experimental import pallas as pl
from jax.experimental.pallas import tpu as pltpu
from jax.sharding import PartitionSpec as P

MESH = pl.DeviceIdType.MESH
F32 = jnp.float32
BF16 = jnp.bfloat16
BS = 1024
K = 128
ROWS = 8
COLS = 16
CH = 256
NC = BS // CH
GROUP = 640
PARTS = ((0, 16, "yzx"), (16, 16, "zxy"), (32, 8, "xyz"))


def split(v):
    high = v.astype(BF16)
    return high, (v - high.astype(F32)).astype(BF16)


def both(v):
    return jnp.concatenate(split(v), axis=1)


def dot(a, b):
    return jnp.dot(a, b, preferred_element_type=F32)


def product(high, low, pair):
    wide = dot(high, pair)
    return wide[:, :K] + wide[:, K:] + dot(low, pair[:, :K])


def chunk(c):
    return pl.ds(pl.multiple_of(c * CH, CH), CH)


def kernel(
    band_in, marginal, penalty_in, ld_diag, ld_low, genotypes,
    effects, scores,
    band, stage, diag_stage, tiles, flipped, geno, vec, m1, m2, via, pair, tail, u2, ru2, us, rus, look, dw,
    penalty, q1, r1, d1, d2, x01, rounded, payload, ar_one, ar_two, mid,
    sc, rc, total, p0a, p0b, p0c, p1a, p1b, p1c, p2a, p2b, p2c, v0, v1, v2, w0, w1, w2, mine40,
    small_sem, load_sem, diag_sem, geno_sem, out_sem, chain_s, chain_r, up_r, via_r, ar_s, ar_r, core_s, core_r,
    rs_s, rs_r,
):
    row, col = lax.axis_index("row"), lax.axis_index("col")
    place = row * COLS + col
    y, core, x, z = row // 2, row % 2, col // 4, col % 4

    def hop(distance):
        to = (place + distance + ROWS * COLS) % (ROWS * COLS)
        return (to // COLS, to % COLS)

    def at(**new):
        p = dict(y=y, core=core, x=x, z=z)
        p.update(new)
        return (p["y"] * 2 + p["core"], p["x"] * 4 + p["z"])

    back = at(z=(z + 3) % 4)
    onward = hop(jnp.where(z == 3, -1, 3))
    from_onward = hop(jnp.where(z == 2, 1, -3))

    b_copy = pltpu.make_async_copy(marginal, vec.at[0], small_sem.at[0])
    band_copy = pltpu.make_async_copy(band_in, band, small_sem.at[2])
    penalty_copy = pltpu.make_async_copy(penalty_in, penalty, small_sem.at[1])
    geno_copy = pltpu.make_async_copy(genotypes, geno, geno_sem)

    def load(t, c):
        return pltpu.make_async_copy(ld_low.at[0, 1 - t, :, chunk(c)], stage.at[c], load_sem.at[c])

    diag_copy = pltpu.make_async_copy(ld_diag.at[0], diag_stage, diag_sem)

    band_copy.start()
    b_copy.start()
    penalty_copy.start()
    for c in range(NC):
        load(0, c).start()

    barrier = pltpu.get_barrier_semaphore()
    for device in (hop(1), hop(2), hop(-1), hop(-2), onward, from_onward):
        pl.semaphore_signal(barrier, inc=1, device_id=device, device_id_type=MESH)

    @pl.loop(1, COLS)
    def _(k):
        pl.semaphore_signal(barrier, inc=1, device_id=(row, (col + k) % COLS), device_id_type=MESH)

    @pl.loop(1, ROWS)
    def _(k):
        pl.semaphore_signal(barrier, inc=1, device_id=((row + k) % ROWS, col), device_id_type=MESH)

    b_copy.wait()
    band_copy.wait()
    pl.semaphore_wait(barrier, 6 + COLS - 1 + ROWS - 1)

    def remote(src, dst, send, recv, device):
        return pltpu.make_async_remote_copy(
            src_ref=src, dst_ref=dst, send_sem=send, recv_sem=recv,
            device_id=device, device_id_type=MESH,
        )

    def send_own(e, c):
        return remote(vec.at[e, chunk(c)], m1.at[e, chunk(c)],
                      chain_s.at[0], chain_r.at[e, 0, c], hop(1))

    def send_on(e, c):
        return remote(m1.at[e, chunk(c)], m2.at[e, chunk(c)],
                      chain_s.at[1 if e < 2 else 2], chain_r.at[e, 1, c], hop(1))

    def send_u2(e, c):
        return remote(u2.at[e, chunk(c)], ru2.at[e, chunk(c)],
                      chain_s.at[3], up_r.at[e, 0, c], hop(-1))

    def send_us(e, c):
        return remote(us.at[e, chunk(c)], rus.at[e, chunk(c)],
                      chain_s.at[4], up_r.at[e, 1, c], hop(-1))

    def send_back(c):
        return remote(vec.at[2, chunk(c)], via.at[chunk(c)],
                      chain_s.at[5], via_r.at[c - 2], back)

    def send_onward(c):
        return remote(via.at[chunk(c)], m2.at[2, chunk(c)],
                      chain_s.at[6], chain_r.at[2, 1, c], onward)

    @pl.loop(0, NC)
    def _(c):
        send_own(0, c).start()

    diag_copy.start()

    place_f = [place >= distance for distance in (1, 2)]
    active = [
        jnp.where(jnp.logical_and(place_f[d - 1], band[0] >= d), 1.0, 0.0).astype(F32) for d in (1, 2)
    ]

    def convert(t, c):
        load(t, c).wait()
        block = stage[c] * active[1 - t]
        high, low = split(block)
        tiles[t, 0, :, chunk(c)] = high
        tiles[t, 1, :, chunk(c)] = low
        high, low = split(block.T)
        flipped[t, 0, chunk(c), :] = high
        flipped[t, 1, chunk(c), :] = low
        if t == 0:
            load(1, c).start()

    def ar_copy(n, step, k):
        if step == 0:
            return remote(payload.at[n], ar_one.at[n, k - 1], ar_s.at[0], ar_r.at[n, 0], (row, (col + k) % COLS))
        return remote(mid.at[n], ar_two.at[n, k - 1], ar_s.at[1], ar_r.at[n, 1], ((row + k) % ROWS, col))

    def ar_all(n, step):
        ref = (ar_one, ar_two)[step].at[n]
        return remote(ref, ref, ar_s.at[step], ar_r.at[n, step], hop(1))

    def ar_send(n, step):
        @pl.loop(1, (COLS, ROWS)[step])
        def _(k):
            ar_copy(n, step, k).start()

    def ar_start(n, rows):
        for j in range(8):
            payload[n, j : j + 1, :] = rows[j] if j < len(rows) else jnp.zeros((1, K), F32)
        ar_send(n, 0)

    def ar_sum(n, step):
        ar_all(n, step).wait_recv()
        acc = (payload, mid)[step][n]
        for k in range(1, (COLS, ROWS)[step]):
            acc = acc + (ar_one, ar_two)[step][n, k - 1]
        return acc

    def ar_next(n):
        mid[n] = ar_sum(n, 0)
        ar_send(n, 1)

    def column(v):
        return jnp.sum(v, axis=0, keepdims=True)

    def over_chunks(body, count):
        zero = jnp.zeros((1, K), F32)
        return lax.fori_loop(0, NC, body, (zero,) * count)

    def add_second(e, c):
        there = both(m2[e, chunk(c), :])
        for r in range(NC):
            rows = pl.ds(r * CH, CH)
            look[e, rows, :] += product(tiles[0, 0, rows, chunk(c)], tiles[0, 1, rows, chunk(c)], there)

    def add_first(e, c):
        there = both(m1[e, chunk(c), :])
        for r in range(NC):
            rows = pl.ds(r * CH, CH)
            part = product(tiles[1, 0, rows, chunk(c)], tiles[1, 1, rows, chunk(c)], there)
            look[e, rows, :] = jnp.where(c == 0, part, part + look[e, rows, :])

    def below(e, r, last):
        return look[e, chunk(r), :] + product(
            tiles[0, 0, chunk(r), chunk(last)], tiles[0, 1, chunk(r), chunk(last)], tail[...]
        )

    def diagonal(e):
        if e == 0:
            diag_copy.wait()

        @pl.loop(0, NC)
        def _(c):
            if e == 0:
                high, low = split(diag_stage[chunk(c), :])
                tiles[2, 0, chunk(c), :] = high
                tiles[2, 1, chunk(c), :] = low
            dw[chunk(c), :] = (
                product(tiles[2, 0, chunk(c), :], tiles[2, 1, chunk(c), :], pair[...])
                + penalty[...] * vec[e, chunk(c), :]
            )

    def exchange(e, early, middle, between, late):
        @pl.loop(0, NC)
        def _(c):
            if e == 0:
                convert(0, c)
            u2[e, chunk(c), :] = product(flipped[0, 0, chunk(c), :], flipped[0, 1, chunk(c), :], pair[...])
            send_u2(e, c).start()

        early()

        @pl.loop(0, NC)
        def _(c):
            send_own(e, c).wait_recv()
            send_on(e, c).start()
            if e == 0:
                convert(1, c)
            up = product(flipped[1, 0, chunk(c), :], flipped[1, 1, chunk(c), :], pair[...])
            send_u2(e, c).wait_recv()
            us[e, chunk(c), :] = up + ru2[e, chunk(c), :]
            send_us(e, c).start()
            add_first(e, c)

        middle()
        diagonal(e)
        between()

        @pl.loop(0, NC - 1)
        def _(c):
            send_on(e, c).wait_recv()
            add_second(e, c)

        late()
        send_on(e, NC - 1).wait_recv()
        tail[...] = both(m2[e, chunk(NC - 1), :])

    def finish(e, c):
        down = below(e, c, NC - 1)
        part = dw[chunk(c), :]
        send_us(e, c).wait_recv()
        out = part + down + rus[e, chunk(c), :]
        vec[e + 1, chunk(c), :] = out
        send_own(e + 1, c).start()
        look[e, chunk(c), :] = part + 2.0 * down
        pair[chunk(c), :] = both(out)
        return out

    @pl.loop(0, NC)
    def _(c):
        pair[chunk(c), :] = both(vec[0, chunk(c), :])

    penalty_copy.wait()
    exchange(0, lambda: None, geno_copy.start, lambda: None, lambda: None)

    def one(c, sums):
        out = finish(0, c)
        here = vec[0, chunk(c), :]
        return (sums[0] + column(here * here), sums[1] + column(here * out), sums[2] + column(out * out))

    sums_one = over_chunks(one, 3)

    coef = {}

    def late_one():
        got = ar_sum(0, 1)
        bb, bq, qq = got[0:1], got[1:2], got[2:3]
        alpha = bb / bq
        after = jnp.maximum(bb - 2.0 * alpha * bq + alpha * alpha * qq, 0.0)
        coef["a0"], coef["b1"] = alpha, after / bb

    exchange(1, lambda: ar_start(0, sums_one), lambda: ar_next(0), lambda: None, lambda: None)

    @pl.loop(0, NC)
    def _(c):
        finish(1, c)

    for c in (2, 3):
        send_back(c).start()
    late_one()
    a0, b1 = coef["a0"], coef["b1"]

    def two(c, sums):
        here, q, s = vec[0, chunk(c), :], vec[1, chunk(c), :], vec[2, chunk(c), :]
        res = here - a0 * q
        direction = res + b1 * here
        image = (1.0 + b1) * q - a0 * s
        r1[chunk(c), :] = res
        d1[chunk(c), :] = direction
        q1[chunk(c), :] = image
        terms = (res * res, res * direction, direction * image, res * image, image * image)
        return tuple(t + column(v) for t, v in zip(sums, terms))

    sums_two = over_chunks(two, 5)
    ar_start(1, sums_two)

    for c in range(NC):
        send_own(2, c).wait_recv()
        if c < 2:
            send_on(2, c).start()
        else:
            send_back(c).wait_recv()
            send_onward(c).start()
        add_first(2, c)
    ar_next(1)
    diagonal(2)
    for c in (2, 3):
        send_onward(c).wait_recv()
        add_second(2, c)
    send_on(2, 0).wait_recv()
    add_second(2, 0)
    got = ar_sum(1, 1)
    rr, rd, dq, rq, qq = (got[j : j + 1] for j in range(5))
    a1 = rd / dq
    after = jnp.maximum(rr - 2.0 * a1 * rq + a1 * a1 * qq, 0.0)
    b2 = after / rr

    def update(c, sums):
        res = r1[chunk(c), :] - a1 * q1[chunk(c), :]
        direction = res + b2 * d1[chunk(c), :]
        d2[chunk(c), :] = direction
        x01[chunk(c), :] = a0 * vec[0, chunk(c), :] + a1 * d1[chunk(c), :]
        return (sums[0] + column(res * direction),)

    rd2 = over_chunks(update, 1)[0]
    c0 = 1.0 + b2 * (1.0 + b1)
    c1 = -a0 - a1 * (1.0 + b1) - b2 * a0
    c2 = a1 * a0

    send_on(2, 1).wait_recv()
    tail[...] = both(m2[2, chunk(1), :])

    def three(c, sums):
        third = dw[chunk(c), :] + 2.0 * below(2, c, 1)
        image = c0 * look[0, chunk(c), :] + c1 * look[1, chunk(c), :] + c2 * third
        return (sums[0] + column(d2[chunk(c), :] * image),)

    dq2 = over_chunks(three, 1)[0]
    ar_start(2, (rd2, dq2))
    geno_copy.wait()
    ar_next(2)
    got = ar_sum(2, 1)
    a2 = got[0:1] / got[1:2]

    @pl.loop(0, NC)
    def _(c):
        value = x01[chunk(c), :] + a2 * d2[chunk(c), :]
        x01[chunk(c), :] = value
        rounded[chunk(c), :] = value.astype(BF16)

    effects_copy = pltpu.make_async_copy(x01, effects, out_sem.at[0])
    effects_copy.start()

    def people(j, which):
        rows = pl.ds(pl.multiple_of((j * 2 + which) * GROUP, GROUP), GROUP)
        return dot(geno[rows, :], rounded[...]).reshape(4, 4, 40, K)

    def core_copy(j):
        return remote(sc.at[j], rc.at[j], core_s, core_r.at[j], at(core=1 - core))

    def rows_of(part):
        return pl.ds(PARTS[part][0], PARTS[part][1])

    def first_y(k):
        to = (y + k) % 4
        return remote(total.at[to, :, :, rows_of(0), :], p0a.at[k - 1], rs_s.at[0, 0], rs_r.at[0, 0], at(y=to))

    def first_z(j, k):
        to = (z + k) % 4
        return remote(total.at[j, :, to, rows_of(1), :], p1a.at[k - 1, j], rs_s.at[0, 1], rs_r.at[0, 1], at(z=to))

    def first_x(j, k):
        to = (x + k) % 4
        return remote(total.at[j, to, :, rows_of(2), :], p2a.at[k - 1, j], rs_s.at[0, 2], rs_r.at[0, 2], at(x=to))

    def other_core(n):
        j = (y + n) % 4
        sc[j] = people(j, 1 - core)
        core_copy(j).start()

    def own_core(n):
        j = (y + n) % 4
        mine = people(j, core)
        core_copy(j).wait_recv()
        total[j] = mine + rc[j]
        if n > 0:
            first_y(n).start()
        for k in (1, 3, 2):
            first_z(j, k).start()
            first_x(j, k).start()

    other_core(1)
    other_core(3)
    own_core(1)
    other_core(2)
    own_core(3)
    other_core(0)
    own_core(2)
    own_core(0)

    landed = ((p0a, p0b, p0c), (p1a, p1b, p1c), (p2a, p2b, p2c))
    halfway = ((v0, w0), (v1, w1), (v2, w2))

    def axis_copy(step, part, k):
        order = PARTS[part][2]
        axis = order[step]
        to = (dict(y=y, x=x, z=z)[axis] + k) % 4
        ref = halfway[part][step - 1]
        left = [a for a in "yxz" if a != order[0]]
        src = ref.at[:, to] if step == 1 and left[1] == axis else ref.at[to]
        return remote(src, landed[part][step].at[k - 1], rs_s.at[step, part], rs_r.at[step, part], at(**{axis: to}))

    def landing(step, part):
        ref = landed[part][step]
        return remote(ref, ref, rs_s.at[step, part], rs_r.at[step, part], hop(1))

    def send_axis(step, part):
        for k in (1, 3, 2):
            axis_copy(step, part, k).start()

    for part in (2, 0, 1):
        acc = (
            lambda: total[y, :, :, rows_of(0), :],
            lambda: total[:, :, z, rows_of(1), :],
            lambda: total[:, x, :, rows_of(2), :],
        )[part]()
        landing(0, part).wait_recv()
        for k in (1, 3, 2):
            acc = acc + landed[part][0][k - 1]
        halfway[part][0][...] = acc
        send_axis(1, part)
    for step in (1, 2):
        for part in (2, 0, 1):
            order = PARTS[part][2]
            axis = order[step]
            mine = dict(y=y, x=x, z=z)[axis]
            ref = halfway[part][step - 1]
            left = [a for a in "yxz" if a != order[0]]
            acc = ref[:, mine] if step == 1 and left[1] == axis else ref[mine]
            landing(step, part).wait_recv()
            for k in (1, 3, 2):
                acc = acc + landed[part][step][k - 1]
            if step == 1:
                halfway[part][1][...] = acc
                send_axis(2, part)
            else:
                mine40[rows_of(part), :] = acc

    scores_copy = pltpu.make_async_copy(mine40, scores, out_sem.at[1])
    scores_copy.start()

    def gone(ref, sem):
        remote(ref, ref, sem, sem, hop(1)).wait_send()

    gone(vec, chain_s.at[0])
    gone(m1.at[pl.ds(0, 2)], chain_s.at[1])
    gone(m1.at[2, pl.ds(0, 2 * CH)], chain_s.at[2])
    gone(u2, chain_s.at[3])
    gone(us, chain_s.at[4])
    gone(via.at[pl.ds(2 * CH, 2 * CH)], chain_s.at[5])
    gone(via.at[pl.ds(2 * CH, 2 * CH)], chain_s.at[6])
    for step, ref in enumerate((ar_one, ar_two)):
        gone(ref, ar_s.at[step])
    gone(sc, core_s)
    for step in range(3):
        for part in range(3):
            gone(landed[part][step], rs_s.at[step, part])
    effects_copy.wait()
    scores_copy.wait()


def copy_out(effects_in, scores_in, effects, scores):
    effects[...] = effects_in[...]
    scores[...] = scores_in[...]


def body(marginal, penalty, ld_diag, ld_low, band, genotypes):
    hbm = pl.BlockSpec(memory_space=pl.ANY)
    big = lambda *lead: pltpu.VMEM((*lead, BS, K), F32)
    parts = []
    for _, size, order in PARTS:
        parts += [pltpu.VMEM((3, 4, 4, size, K), F32), pltpu.VMEM((3, 4, size, K), F32), pltpu.VMEM((3, size, K), F32)]
    dma = pltpu.SemaphoreType.DMA
    shapes = (jax.ShapeDtypeStruct((BS, K), F32), jax.ShapeDtypeStruct((40, K), F32))
    results = pl.pallas_call(
        kernel,
        out_shape=shapes,
        in_specs=[hbm, hbm, hbm, hbm, hbm, hbm],
        out_specs=(hbm, hbm),
        scratch_shapes=[
            pltpu.SMEM((1,), jnp.int32),
            pltpu.VMEM((NC, BS, CH), F32),
            pltpu.VMEM((BS, BS), F32),
            pltpu.VMEM((3, 2, BS, BS), BF16),
            pltpu.VMEM((2, 2, BS, BS), BF16),
            pltpu.VMEM((8 * GROUP, BS), BF16),
            big(3), big(3), big(3), big(),
            pltpu.VMEM((BS, 2 * K), BF16),
            pltpu.VMEM((CH, 2 * K), BF16),
            big(2), big(2), big(2), big(2), big(3), big(),
            pltpu.VMEM((1, K), F32), big(), big(), big(), big(), big(),
            pltpu.VMEM((BS, K), BF16),
            pltpu.VMEM((3, 8, K), F32),
            pltpu.VMEM((3, COLS - 1, 8, K), F32),
            pltpu.VMEM((3, ROWS - 1, 8, K), F32),
            pltpu.VMEM((3, 8, K), F32),
            pltpu.VMEM((4, 4, 4, 40, K), F32),
            pltpu.VMEM((4, 4, 4, 40, K), F32),
            pltpu.VMEM((4, 4, 4, 40, K), F32),
            *parts,
            *[pltpu.VMEM((4, 4, size, K), F32) for _, size, _ in PARTS],
            *[pltpu.VMEM((4, size, K), F32) for _, size, _ in PARTS],
            pltpu.VMEM((40, K), F32),
            dma((3,)), dma((NC,)), dma, dma, dma((2,)),
            dma((7,)), dma((3, 2, NC)), dma((2, 2, NC)), dma((2,)),
            dma((2,)), dma((3, 2)),
            dma, dma((4,)),
            dma((3, 3)), dma((3, 3)),
        ],
        compiler_params=pltpu.CompilerParams(
            collective_id=0, has_side_effects=True, vmem_limit_bytes=63 * 1024 * 1024
        ),
    )(band, marginal, penalty.reshape(1, K), ld_diag, ld_low, genotypes)
    return pl.pallas_call(
        copy_out,
        out_shape=shapes,
    )(*results)


def solution(mesh):
    placed = (
        P(("row", "col"), None),
        P(),
        P(("row", "col"), None, None),
        P(("row", "col"), None, None, None),
        P(("row", "col")),
        P(None, ("row", "col")),
    )
    return jax.shard_map(
        body,
        mesh=mesh,
        in_specs=placed,
        out_specs=(P(("row", "col"), None), P(("row", "col"), None)),
        check_vma=False,
    )
```
